32 devices in a mesh: section: 4 (over x, core), dp: 8 (over z, y).
Axes of the slice: x: 2, y: 2, z: 4, core: 2. Of those that a mesh axis runs over, the one named last changes fastest.
Arguments:
- section_inputs: bfloat16 [4, 4, 1024, 2048], P('section', None, 'dp'), may hold values from -8 to 8
- top_grads: bfloat16 [4, 1024, 2048], P(None, 'dp'), may hold values from -8 to 8
- query_weight: bfloat16 [4, 2048, 1024], P('section'), may hold values from -0.375 to 0.375
- output_weight: bfloat16 [4, 2048, 1024], P('section'), may hold values from -0.125 to 0.125
- neighbour_kv: bfloat16 [4, 16, 2, 128, 1024], P('section', 'dp'), may hold values from -6 to 6
- nbr_ids: int32 [4, 16, 2], P(None, 'dp'), may hold values from 0 to 15, as said below
- send_list: int32 [8, 8], replicated, may hold values from 0 to 1, as said below
- send_counts: int32 [8, 8], replicated, may hold values from 0 to 1, as said below
Outputs:
- input_grads: bfloat16 [4, 4, 1024, 2048], P('section', None, 'dp')
- query_grads: bfloat16 [4, 2048, 1024], P('section', 'dp')
- output_grads: bfloat16 [4, 2048, 1024], P('section', 'dp')
- kv_grads: bfloat16 [4, 16, 2, 128, 1024], P('section', 'dp')
The draws below stay inside these ranges and needn't reach their ends.
Inputs may be any that keep to these rules, and one draw needn't show every extreme that they name: `nbr_ids`: the 2 neighbours of a span have different owners. Every neighbour of reader r's spans owned by o is block o * 2 + send_list[o, r]. `send_list`: entry [o, r] is 0 where send_counts[o, r] is 0. `send_counts`: entry [o, r] is 1 where some span of reader r has a neighbour of owner o, else 0.
All inputs are finite; a program needn't handle non-finite values.
Results may differ from the reference program's by a relative error of at most 0.039.
Values may be sent and summed in bfloat16 or wider, within the bound.
No kernel may reach another device: no remote copies, remote signals or barrier semaphores. Data moves between devices by JAX's collectives and lax.ppermute only.
A program may use at most 192 MiB of HBM per device.

```python
import jax
import jax.numpy as jnp
from jax import lax

D = 2048
HEADS = 16
HEAD_DIM = 64
SPAN = 64
K_NBR = 2
NBR_LEN = 128
MICRO = 4
CH_DEV = 2
BLK_DEV = 2
HD = 1024
TOKENS = 1024
SPANS = 16
BLOCKS = 16
SECTIONS = 4
N_DP = 8


def neighbour_plan(key):
    base_key = jax.random.fold_in(key, 7)
    owner_order = jax.random.permutation(jax.random.fold_in(base_key, 1), N_DP)
    rank_one = jax.random.randint(jax.random.fold_in(base_key, 2), (MICRO, SPANS), 0, N_DP)
    rank_two = jax.random.randint(jax.random.fold_in(base_key, 3), (MICRO, SPANS), 0, N_DP)
    first_rank = jnp.minimum(rank_one, rank_two)
    offset_rank = jax.random.randint(jax.random.fold_in(base_key, 4), (MICRO, SPANS), 0, N_DP - 1)
    second_rank = (first_rank + 1 + offset_rank) % N_DP
    owners = owner_order[jnp.stack([first_rank, second_rank], axis=-1)].astype(jnp.int32)
    block_choice = jax.random.randint(jax.random.fold_in(base_key, 5), (N_DP, N_DP), 0, BLK_DEV)
    grouped = owners.reshape(MICRO, N_DP, CH_DEV * K_NBR)
    named = jnp.any(grouped[..., None] == jnp.arange(N_DP, dtype=jnp.int32), axis=(0, 2))
    counts = jnp.transpose(named).astype(jnp.int32)
    lists = (block_choice * counts).astype(jnp.int32)
    reader_of = (jnp.arange(SPANS, dtype=jnp.int32) // CH_DEV)[None, :, None]
    reader_of = jnp.broadcast_to(reader_of, owners.shape)
    ids = (owners * BLK_DEV + lists[owners, reader_of]).astype(jnp.int32)
    return (ids, lists, counts)


def draw_nbr_ids(key, part):
    return neighbour_plan(key)[0]


def draw_send_list(key, part):
    return neighbour_plan(key)[1]


def draw_send_counts(key, part):
    return neighbour_plan(key)[2]


def strengthened(values, stream_key, source, target, blocks, factor):
    owner, partner = [(jnp.arange(values.shape[axis_at]) // (values.shape[axis_at] // blocks)).reshape([-1 if axis == axis_at else 1 for axis in range(values.ndim)]) for axis_at in (source, target)]
    chosen = jax.random.permutation(stream_key, blocks)[partner]
    strong = (owner == chosen) | (owner == (partner + blocks // 2) % blocks)
    return jnp.where(strong, factor * values, values)


def block_levels(own_key, extent, shards, low, top_value):
    level = 1.0
    for axis_at, parts in shards:
        draws = jax.random.uniform(jax.random.fold_in(jax.random.fold_in(own_key, 6), axis_at), (parts,), jnp.float32, low / len(shards), top_value / len(shards))
        level = level * jnp.repeat(jnp.exp(draws), extent[axis_at] // parts).reshape((-1,) + (1,) * (len(extent) - 1 - axis_at))
    return level


def gaussian(own_key, shape, deviation, most, pieces=(), kind=jnp.bfloat16):
    result = jax.random.normal(own_key, shape, jnp.float32) * deviation
    if len(pieces) > 0:
        result = block_levels(own_key, shape, pieces, -0.22, 0.18) * result
    return jnp.clip(result, min=-most, max=most).astype(kind)


def bell_draw_with(stream_key, extent, scale, most, pieces, heavy, kind=jnp.bfloat16):
    result = scale * jax.random.normal(stream_key, extent, jnp.float32)
    if pieces:
        result = result * block_levels(stream_key, extent, pieces, -0.22, 0.18)
    return jnp.clip(strengthened(result, jax.random.fold_in(stream_key, 3), *heavy), -most, most).astype(kind)


def setup_inputs(seed: int = 0) -> dict:
    key_of = jax.random.split(jax.random.key(seed), 9)
    return {
        "section_inputs": bell_draw_with(key_of[0], (SECTIONS, MICRO, TOKENS, D), 1.0, 8.0, ((0, 4), (2, 8)), (2, 3, 8, 2.0)),
        "top_grads": bell_draw_with(key_of[1], (MICRO, TOKENS, D), 1.0, 8.0, ((1, 8),), (1, 2, 8, 2.0)),
        "query_weight": gaussian(key_of[2], (SECTIONS, D, HD), (3.0 * D ** -0.5), 0.375, ((0, 4),)),
        "output_weight": gaussian(key_of[3], (SECTIONS, D, HD), D ** -0.5, 0.125, ((0, 4),)),
        "neighbour_kv": gaussian(key_of[4], (SECTIONS, BLOCKS, 2, NBR_LEN, HD), 1.0, 6.0, ((0, 4), (1, 8))),
        "nbr_ids": draw_nbr_ids(jax.random.fold_in(key_of[8], 71), 0),
        "send_list": draw_send_list(jax.random.fold_in(key_of[8], 71), 0),
        "send_counts": draw_send_counts(jax.random.fold_in(key_of[8], 71), 0),
    }


highest = lax.Precision.HIGHEST


def section_grads(inputs, upstream, query_proj, output_proj, owned_pool, nbr_ids, send_list, send_counts):
    micro_count, token_count, model_width = inputs.shape
    inner_width = HEADS * HEAD_DIM
    span_count = token_count // SPAN
    reader_count = span_count // CH_DEV
    score_scale = HEAD_DIM ** -0.5
    owner_of = nbr_ids // BLK_DEV
    reader_of = jnp.broadcast_to((jnp.arange(span_count, dtype=jnp.int32) // CH_DEV)[None, :, None], owner_of.shape)
    local_block = send_list[owner_of, reader_of]
    mask_value = send_counts[owner_of, reader_of].astype(jnp.float32)
    block_index = (owner_of * BLK_DEV + local_block).astype(jnp.int32)
    picked = (owned_pool[block_index].astype(jnp.float32) * mask_value[..., None, None, None]).astype(jnp.bfloat16)
    key_rows = picked[:, :, :, 0].reshape(micro_count, span_count, K_NBR * NBR_LEN, HEADS, HEAD_DIM).astype(jnp.float32)
    value_rows = picked[:, :, :, 1].reshape(micro_count, span_count, K_NBR * NBR_LEN, HEADS, HEAD_DIM).astype(jnp.float32)
    input_rows = inputs.reshape(-1, model_width)
    query_rows = jnp.dot(input_rows, query_proj, preferred_element_type=jnp.float32).astype(jnp.bfloat16)
    heads_q = lax.optimization_barrier(query_rows).astype(jnp.float32).reshape(micro_count, span_count, SPAN, HEADS, HEAD_DIM)
    scores = jnp.einsum("mcqhd,mckhd->mchqk", heads_q, key_rows, precision=highest) * score_scale
    weights = jnp.exp(scores - jnp.max(scores, axis=-1, keepdims=True))
    probability = weights / jnp.sum(weights, axis=-1, keepdims=True)
    prob_rounded = lax.optimization_barrier(probability.astype(jnp.bfloat16)).astype(jnp.float32)
    attended = jnp.einsum("mchqk,mckhd->mcqhd", prob_rounded, value_rows, precision=highest).astype(jnp.bfloat16)
    attended_rows = attended.reshape(-1, inner_width)
    upstream_rows = upstream.reshape(-1, model_width)
    d_attended = jnp.dot(upstream_rows, output_proj, preferred_element_type=jnp.float32).astype(jnp.bfloat16)
    heads_d = lax.optimization_barrier(d_attended).astype(jnp.float32).reshape(micro_count, span_count, SPAN, HEADS, HEAD_DIM)
    d_probs = jnp.einsum("mcqhd,mckhd->mchqk", heads_d, value_rows, precision=highest)
    row_delta = jnp.sum(probability * d_probs, axis=-1, keepdims=True)
    d_scores = (probability * (d_probs - row_delta) * score_scale).astype(jnp.bfloat16)
    d_scores = lax.optimization_barrier(d_scores).astype(jnp.float32)
    d_query = jnp.einsum("mchqk,mckhd->mcqhd", d_scores, key_rows, precision=highest).astype(jnp.bfloat16)
    d_keys = jnp.einsum("mchqk,mcqhd->mckhd", d_scores, heads_q, precision=highest)
    d_values = jnp.einsum("mchqk,mcqhd->mckhd", prob_rounded, heads_d, precision=highest)
    d_rows = d_query.reshape(-1, inner_width)
    grads_in = (upstream_rows.astype(jnp.float32) + jnp.dot(d_rows, query_proj.T, preferred_element_type=jnp.float32)).astype(jnp.bfloat16)
    grads_in = grads_in.reshape(micro_count, token_count, model_width)
    flat_size = 2 * NBR_LEN * inner_width
    per_ref = jnp.stack([d_keys.reshape(micro_count, span_count, K_NBR, NBR_LEN * inner_width), d_values.reshape(micro_count, span_count, K_NBR, NBR_LEN * inner_width)], axis=3)
    per_ref = per_ref.reshape(micro_count, reader_count, CH_DEV, K_NBR, flat_size)
    owner_pick = (owner_of[..., None] == jnp.arange(N_DP, dtype=jnp.int32)).astype(jnp.float32)
    owner_pick = owner_pick.reshape(micro_count, reader_count, CH_DEV, K_NBR, N_DP)
    partial_value = jnp.einsum("mrjko,mrjkf->rof", owner_pick, per_ref, precision=highest).astype(jnp.bfloat16)
    partial_value = lax.optimization_barrier(partial_value).astype(jnp.float32)
    own_pick = (send_list[:, :, None] == jnp.arange(BLK_DEV, dtype=jnp.int32)).astype(jnp.float32) * send_counts[:, :, None].astype(jnp.float32)
    kv_grad = jnp.einsum("orb,rof->obf", own_pick, partial_value, precision=highest).astype(jnp.bfloat16)
    kv_grad = kv_grad.reshape(N_DP * BLK_DEV, 2, NBR_LEN, inner_width)
    grad_scale = (micro_count * token_count) ** -0.5
    input_f = inputs.astype(jnp.float32).reshape(micro_count, reader_count, -1, model_width)
    query_f = d_rows.astype(jnp.float32).reshape(micro_count, reader_count, -1, inner_width)
    query_terms = (jnp.einsum("mrtd,mrte->rde", input_f, query_f, precision=highest) * grad_scale).astype(jnp.bfloat16)
    query_grad = jnp.sum(lax.optimization_barrier(query_terms).astype(jnp.float32), axis=0).astype(jnp.bfloat16)
    upstream_f = upstream.astype(jnp.float32).reshape(micro_count, reader_count, -1, model_width)
    attended_f = attended_rows.astype(jnp.float32).reshape(micro_count, reader_count, -1, inner_width)
    output_terms = (jnp.einsum("mrtd,mrte->rde", upstream_f, attended_f, precision=highest) * grad_scale).astype(jnp.bfloat16)
    output_grad = jnp.sum(lax.optimization_barrier(output_terms).astype(jnp.float32), axis=0).astype(jnp.bfloat16)
    return grads_in, query_grad, output_grad, kv_grad


def reference(section_inputs, top_grads, query_weight, output_weight, neighbour_kv, nbr_ids, send_list, send_counts):
    def section_step(upstream, section_items):
        inputs, query_proj, output_proj, owned_pool = section_items
        grads_in, query_grad, output_grad, kv_grad = section_grads(inputs, upstream, query_proj, output_proj, owned_pool, nbr_ids, send_list, send_counts)
        return grads_in, (grads_in, query_grad, output_grad, kv_grad)

    final_grad, stacked = lax.scan(section_step, top_grads, (section_inputs, query_weight, output_weight, neighbour_kv), reverse=True)
    input_grads, query_grads, output_grads, kv_grads = stacked
    return (input_grads, query_grads, output_grads, kv_grads)
```

```python
import functools

import jax
import jax.numpy as jnp
from jax import lax
from jax.experimental import pallas as pl
from jax.experimental.pallas import tpu as pltpu
from jax.sharding import PartitionSpec as P

HEADS = 16
HEAD_DIM = 64
SPAN = 64
K_NBR = 2
NBR_LEN = 128
PAIR = 2 * HEAD_DIM
KEYS = K_NBR * NBR_LEN
SCALE = HEAD_DIM ** (-0.5)
BF = jnp.bfloat16
F32 = jnp.float32
ANY = pl.BlockSpec(memory_space=pl.ANY)


def nt(a, b):
    return lax.dot_general(a, b, (((1,), (1,)), ((), ())), preferred_element_type=F32)


def nn(a, b):
    return lax.dot_general(a, b, (((1,), (0,)), ((), ())), preferred_element_type=F32)


def tn(a, b):
    return lax.dot_general(a, b, (((0,), (0,)), ((), ())), preferred_element_type=F32)


def head_rows(x):
    heads = x.shape[1] // HEAD_DIM
    if heads == 1:
        return x
    lane = lax.broadcasted_iota(jnp.int32, x.shape, 1) // HEAD_DIM
    zero = jnp.zeros_like(x)
    return jnp.concatenate([jnp.where(lane == h, x, zero) for h in range(heads)], axis=0)


def head_columns(y):
    heads = y.shape[1] // HEAD_DIM
    out = y[:SPAN]
    lane = lax.broadcasted_iota(jnp.int32, out.shape, 1) // HEAD_DIM
    for h in range(1, heads):
        out = jnp.where(lane == h, y[h * SPAN : (h + 1) * SPAN], out)
    return out


def softmax_rows(scores):
    weights = jnp.exp(scores - jnp.max(scores, axis=-1, keepdims=True))
    return weights / jnp.sum(weights, axis=-1, keepdims=True)


def probs_kernel(owners, q_ref, k_ref, out_ref):
    micro = pl.program_id(0)
    tokens, width = q_ref.shape[1], q_ref.shape[2]
    spans = tokens // SPAN
    for span in range(spans):
        refs = [owners[(micro * spans + span) * K_NBR + k] for k in range(K_NBR)]
        for pair in range(width // PAIR):
            cols = slice(pair * PAIR, (pair + 1) * PAIR)
            keys = jnp.concatenate([k_ref[r, :, cols] for r in refs], axis=0)
            rows = head_rows(q_ref[0, span * SPAN : (span + 1) * SPAN, cols])
            out_ref[0, span * (width // PAIR) + pair] = softmax_rows(nt(rows, keys) * SCALE).astype(BF)


def tick_kernel(
    chunks,
    scal,
    arriving, top, w_out, w_query, keys, values, probs, g0, q0, a0, u0, d0,
    leaving, g_store, q_store, a_store, u_store, d_store,
    up, wo, wq, kb, vb, pb, datt, dq, att, gr, sem_up, sem_wo, sem_wq, sem_k, sem_v, sem_p, sem_out,
):
    micro = scal[0]
    valid = scal[1]
    last = scal[2]
    tokens = up.shape[0]
    spans = tokens // SPAN
    refs = spans * K_NBR
    pairs = datt.shape[1] // PAIR
    rows = w_out.shape[0] // chunks

    def copy_wo(c):
        return pltpu.make_async_copy(w_out.at[pl.ds(c * rows, rows)], wo.at[c], sem_wo.at[c])

    def copy_wq(c):
        return pltpu.make_async_copy(w_query.at[pl.ds(c * rows, rows)], wq.at[c], sem_wq.at[c])

    def copy_v(i):
        return pltpu.make_async_copy(values.at[scal[3 + i]], vb.at[i], sem_v.at[i])

    def copy_k(i):
        return pltpu.make_async_copy(keys.at[scal[3 + i]], kb.at[i], sem_k.at[i])

    @pl.when(valid > 0)
    def _():
        from_top = pltpu.make_async_copy(top.at[micro], up, sem_up)
        from_hop = pltpu.make_async_copy(arriving, up, sem_up)

        @pl.when(last > 0)
        def _():
            from_top.start()

        @pl.when(last == 0)
        def _():
            from_hop.start()

        for c in range(chunks):
            copy_wo(c).start()
        for i in range(refs):
            copy_v(i).start()
        get_probs = pltpu.make_async_copy(probs.at[micro], pb, sem_p)
        get_probs.start()
        for i in range(refs):
            copy_k(i).start()
        for c in range(chunks):
            copy_wq(c).start()
        from_hop.wait()
        save_up = pltpu.make_async_copy(up, u_store.at[micro], sem_out.at[0])
        save_up.start()
        acc = None
        for c in range(chunks):
            copy_wo(c).wait()
            part = nn(up[:, c * rows : (c + 1) * rows], wo[c])
            acc = part if acc is None else acc + part
        datt[...] = acc.astype(BF)
        save_d = pltpu.make_async_copy(datt, d_store.at[micro], sem_out.at[1])
        save_d.start()
        for i in range(refs):
            copy_v(i).wait()
        get_probs.wait()
        for i in range(refs):
            copy_k(i).wait()
        for span in range(spans):
            rws = slice(span * SPAN, (span + 1) * SPAN)
            for pair in range(pairs):
                cols = slice(pair * PAIR, (pair + 1) * PAIR)
                val = jnp.concatenate([vb[span * K_NBR + k, :, cols] for k in range(K_NBR)], axis=0)
                key = jnp.concatenate([kb[span * K_NBR + k, :, cols] for k in range(K_NBR)], axis=0)
                prob_b = pb[span * pairs + pair]
                d_probs = nt(head_rows(datt[rws, cols]), val)
                prob = prob_b.astype(F32)
                delta = jnp.sum(prob * d_probs, axis=-1, keepdims=True)
                d_scores = (prob * (d_probs - delta) * SCALE).astype(BF)
                dq[rws, cols] = head_columns(nn(d_scores, key)).astype(BF)
                att[rws, cols] = head_columns(nn(prob_b, val)).astype(BF)
        save_q = pltpu.make_async_copy(dq, q_store.at[micro], sem_out.at[2])
        save_q.start()
        save_a = pltpu.make_async_copy(att, a_store.at[micro], sem_out.at[3])
        save_a.start()
        for c in range(chunks):
            copy_wq(c).wait()
            cols = slice(c * rows, (c + 1) * rows)
            gr[:, cols] = (up[:, cols].astype(F32) + nt(dq[...], wq[c])).astype(BF)
        send = pltpu.make_async_copy(gr, leaving, sem_out.at[4])
        send.start()
        save_g = pltpu.make_async_copy(gr, g_store.at[micro], sem_out.at[5])
        save_g.start()
        for c in (save_up, save_d, save_q, save_a, send, save_g):
            c.wait()


def block_grads_kernel(ids, mask, q_ref, d_ref, kv_ref, out_ref, acc):
    reader = pl.program_id(0)
    micros, tokens, width = q_ref.shape[1], q_ref.shape[2], q_ref.shape[3]
    spans = tokens // SPAN
    readers = pl.num_programs(0)

    @pl.when(reader == 0)
    def _():
        acc[...] = jnp.zeros_like(acc)

    for micro in range(micros):
        for span in range(spans):
            at = [((micro * readers + reader) * spans + span) * K_NBR + k for k in range(K_NBR)]
            rws = slice(span * SPAN, (span + 1) * SPAN)
            refs = [ids[i] for i in at]
            keep = [mask[i] > 0 for i in at]
            zero = jnp.zeros((NBR_LEN, width), BF)
            key = jnp.concatenate([jnp.where(m, kv_ref[r, 0], zero) for m, r in zip(keep, refs)], axis=0)
            val = jnp.concatenate([jnp.where(m, kv_ref[r, 1], zero) for m, r in zip(keep, refs)], axis=0)
            q_rows = head_rows(q_ref[0, micro, rws])
            d_rows = head_rows(d_ref[0, micro, rws])
            prob = softmax_rows(nt(q_rows, key) * SCALE)
            d_probs = nt(d_rows, val)
            delta = jnp.sum(prob * d_probs, axis=-1, keepdims=True)
            d_scores = (prob * (d_probs - delta) * SCALE).astype(BF)
            d_keys = tn(d_scores, q_rows)
            d_values = tn(prob.astype(BF), d_rows)
            fzero = jnp.zeros((NBR_LEN, width), F32)
            for k in range(K_NBR):
                part = slice(k * NBR_LEN, (k + 1) * NBR_LEN)
                acc[refs[k], 0] += jnp.where(keep[k], d_keys[part], fzero)
                acc[refs[k], 1] += jnp.where(keep[k], d_values[part], fzero)

    @pl.when(reader == readers - 1)
    def _():
        out_ref[...] = acc[...].astype(BF)


def body(
    section_inputs,
    top_grads,
    query_weight,
    output_weight,
    neighbour_kv,
    nbr_ids,
    send_list,
    send_counts,
):
    n_section = lax.axis_size("section")
    section_index = lax.axis_index("section")
    n_data = lax.axis_size("dp")
    data_index = lax.axis_index("dp")
    inputs_all = section_inputs[0]
    w_query = query_weight[0]
    w_out = output_weight[0]
    owned = neighbour_kv[0]
    micros, tokens, model = inputs_all.shape
    blk_dev = owned.shape[0]
    width = w_query.shape[1]
    spans = tokens // SPAN
    slice_w = width // n_data
    params = functools.partial(pltpu.CompilerParams, vmem_limit_bytes=56 << 20)

    my_list = lax.dynamic_index_in_dim(send_list, data_index, 0, keepdims=False)
    my_counts = lax.dynamic_index_in_dim(send_counts, data_index, 0, keepdims=False)

    def outbound(which):
        picked = jnp.zeros((n_data, NBR_LEN, width), BF)
        for b in range(blk_dev):
            chosen = ((my_list == b) & (my_counts > 0))[:, None, None]
            picked = jnp.where(chosen, owned[b, which][None], picked)
        return picked

    def exchange(x):
        return lax.all_to_all(x, "dp", split_axis=0, concat_axis=0, tiled=True)

    keys = exchange(outbound(0))
    values = exchange(outbound(1))
    query = nn(inputs_all.reshape(micros * tokens, model), w_query).astype(BF)
    query = query.reshape(micros, tokens, width)
    owners = (nbr_ids // blk_dev).astype(jnp.int32)

    probs = pl.pallas_call(
        probs_kernel,
        out_shape=jax.ShapeDtypeStruct((micros, spans * width // PAIR, 2 * SPAN, KEYS), BF),
        grid_spec=pltpu.PrefetchScalarGridSpec(
            num_scalar_prefetch=1,
            grid=(micros,),
            in_specs=[
                pl.BlockSpec((1, tokens, width), lambda i, o: (i, 0, 0)),
                pl.BlockSpec((n_data, NBR_LEN, width), lambda i, o: (0, 0, 0)),
            ],
            out_specs=pl.BlockSpec((1, spans * width // PAIR, 2 * SPAN, KEYS), lambda i, o: (i, 0, 0, 0)),
        ),
        compiler_params=params(),
    )(owners.reshape(-1), query, keys)

    chunks = 4
    lag = 2 * (n_section - 1 - section_index)
    last = (section_index == n_section - 1).astype(jnp.int32)
    refs = spans * K_NBR
    tick = pl.pallas_call(
        functools.partial(tick_kernel, chunks),
        out_shape=(
            jax.ShapeDtypeStruct((tokens, model), BF),
            jax.ShapeDtypeStruct((micros, tokens, model), BF),
            jax.ShapeDtypeStruct((micros, tokens, width), BF),
            jax.ShapeDtypeStruct((micros, tokens, width), BF),
            jax.ShapeDtypeStruct((micros, tokens, model), BF),
            jax.ShapeDtypeStruct((micros, tokens, width), BF),
        ),
        grid_spec=pltpu.PrefetchScalarGridSpec(
            num_scalar_prefetch=1,
            grid=(1,),
            in_specs=[ANY] * 12,
            out_specs=[ANY] * 6,
            scratch_shapes=[
                pltpu.VMEM((tokens, model), BF),
                pltpu.VMEM((chunks, model // chunks, width), BF),
                pltpu.VMEM((chunks, model // chunks, width), BF),
                pltpu.VMEM((refs, NBR_LEN, width), BF),
                pltpu.VMEM((refs, NBR_LEN, width), BF),
                pltpu.VMEM((spans * width // PAIR, 2 * SPAN, KEYS), BF),
                pltpu.VMEM((tokens, width), BF),
                pltpu.VMEM((tokens, width), BF),
                pltpu.VMEM((tokens, width), BF),
                pltpu.VMEM((tokens, model), BF),
                pltpu.SemaphoreType.DMA,
                pltpu.SemaphoreType.DMA((chunks,)),
                pltpu.SemaphoreType.DMA((chunks,)),
                pltpu.SemaphoreType.DMA((refs,)),
                pltpu.SemaphoreType.DMA((refs,)),
                pltpu.SemaphoreType.DMA,
                pltpu.SemaphoreType.DMA((6,)),
            ],
        ),
        input_output_aliases={8: 1, 9: 2, 10: 3, 11: 4, 12: 5},
        compiler_params=params(),
    )
    hop_pairs = [(i, i - 1) for i in range(1, n_section)]

    def run_tick(index, state):
        arriving, leaving, stores = state
        coming = lax.ppermute(leaving, "section", hop_pairs)
        micro_now = index - lag
        valid = ((micro_now >= 0) & (micro_now < micros)).astype(jnp.int32)
        slot = jnp.clip(micro_now, 0, micros - 1)
        mine = lax.dynamic_index_in_dim(owners, slot, 0, keepdims=False).reshape(-1)
        scal = jnp.concatenate([jnp.stack([slot, valid, last]).astype(jnp.int32), mine])
        out = tick(scal, arriving, top_grads, w_out, w_query, keys, values, probs, *stores)
        return coming, out[0], out[1:]

    stores = (
        jnp.zeros((micros, tokens, model), BF),
        jnp.zeros((micros, tokens, width), BF),
        jnp.zeros((micros, tokens, width), BF),
        jnp.zeros((micros, tokens, model), BF),
        jnp.zeros((micros, tokens, width), BF),
    )
    empty = jnp.zeros((tokens, model), BF)
    ticks = micros + 2 * (n_section - 1)
    _, _, stores = lax.fori_loop(0, ticks, run_tick, (empty, empty, stores))
    grads_in, d_query, attended, upstream, d_attended = stores

    flat = micros * tokens
    grad_scale = (flat * n_data) ** (-0.5)
    query_term = tn(inputs_all.reshape(flat, model), d_query.reshape(flat, width))
    output_term = tn(upstream.reshape(flat, model), attended.reshape(flat, width))
    shares = lax.psum_scatter(
        (jnp.concatenate([query_term, output_term], axis=1) * grad_scale).astype(BF),
        "dp",
        scatter_dimension=0,
        tiled=True,
    )

    def by_heads(x):
        lead = x.shape[:-1]
        x = jnp.moveaxis(x.reshape(*lead, n_data, slice_w), -2, 0)
        return exchange(x)

    kv_heads = by_heads(owned).reshape(n_data * blk_dev, 2, NBR_LEN, slice_w)
    q_heads = by_heads(query)
    d_heads = by_heads(d_attended)
    ids_all = lax.all_gather(nbr_ids, "dp", axis=1, tiled=True)
    owner_all = ids_all // blk_dev
    reader_all = (jnp.arange(n_data * spans, dtype=jnp.int32) // spans)[None, :, None]
    hit_owner = owner_all[..., None] == jnp.arange(n_data, dtype=jnp.int32)
    list_r = jnp.take(send_list, reader_all[0, :, 0], axis=1).T[None, :, None, :]
    count_r = jnp.take(send_counts, reader_all[0, :, 0], axis=1).T[None, :, None, :]
    block_all = owner_all * blk_dev + jnp.sum(jnp.where(hit_owner, list_r, 0), axis=-1)
    mask_all = jnp.sum(jnp.where(hit_owner, count_r, 0), axis=-1)
    blocks = n_data * blk_dev
    block_grads = pl.pallas_call(
        block_grads_kernel,
        out_shape=jax.ShapeDtypeStruct((blocks, 2, NBR_LEN, slice_w), BF),
        grid_spec=pltpu.PrefetchScalarGridSpec(
            num_scalar_prefetch=2,
            grid=(n_data,),
            in_specs=[
                pl.BlockSpec((1, micros, tokens, slice_w), lambda i, a, b: (i, 0, 0, 0)),
                pl.BlockSpec((1, micros, tokens, slice_w), lambda i, a, b: (i, 0, 0, 0)),
                pl.BlockSpec((blocks, 2, NBR_LEN, slice_w), lambda i, a, b: (0, 0, 0, 0)),
            ],
            out_specs=pl.BlockSpec((blocks, 2, NBR_LEN, slice_w), lambda i, a, b: (0, 0, 0, 0)),
            scratch_shapes=[pltpu.VMEM((blocks, 2, NBR_LEN, slice_w), F32)],
        ),
        compiler_params=params(),
    )(block_all.reshape(-1).astype(jnp.int32), mask_all.reshape(-1).astype(jnp.int32), q_heads, d_heads, kv_heads)
    returned = exchange(block_grads.reshape(n_data, blk_dev, 2, NBR_LEN, slice_w))
    kv_grads = jnp.moveaxis(returned, 0, -2).reshape(blk_dev, 2, NBR_LEN, width)
    return (
        grads_in[None],
        shares[None, :, :width],
        shares[None, :, width:],
        kv_grads[None],
    )


def solution(mesh):
    in_specs = (
        P("section", None, "dp", None),
        P(None, "dp", None),
        P("section", None, None),
        P("section", None, None),
        P("section", "dp", None, None, None),
        P(None, "dp", None),
        P(),
        P(),
    )
    out_specs = (
        P("section", None, "dp", None),
        P("section", "dp", None),
        P("section", "dp", None),
        P("section", "dp", None, None, None),
    )
    return jax.shard_map(body, mesh=mesh, in_specs=in_specs, out_specs=out_specs, check_vma=False)
```

```python
import functools

import jax
import jax.numpy as jnp
from jax import lax
from jax.experimental import pallas as pl
from jax.experimental.pallas import tpu as pltpu
from jax.sharding import PartitionSpec as P

HEADS = 16
HEAD_DIM = 64
SPAN = 64
K_NBR = 2
NBR_LEN = 128
PAIR = 2 * HEAD_DIM
KEYS = K_NBR * NBR_LEN
SCALE = HEAD_DIM ** (-0.5)
BF = jnp.bfloat16
F32 = jnp.float32
ANY = pl.BlockSpec(memory_space=pl.ANY)


def nt(a, b):
    return lax.dot_general(a, b, (((1,), (1,)), ((), ())), preferred_element_type=F32)


def nn(a, b):
    return lax.dot_general(a, b, (((1,), (0,)), ((), ())), preferred_element_type=F32)


def tn(a, b):
    return lax.dot_general(a, b, (((0,), (0,)), ((), ())), preferred_element_type=F32)


def head_rows(x):
    heads = x.shape[1] // HEAD_DIM
    if heads == 1:
        return x
    lane = lax.broadcasted_iota(jnp.int32, x.shape, 1) // HEAD_DIM
    zero = jnp.zeros_like(x)
    return jnp.concatenate([jnp.where(lane == h, x, zero) for h in range(heads)], axis=0)


def head_columns(y):
    heads = y.shape[1] // HEAD_DIM
    out = y[:SPAN]
    lane = lax.broadcasted_iota(jnp.int32, out.shape, 1) // HEAD_DIM
    for h in range(1, heads):
        out = jnp.where(lane == h, y[h * SPAN : (h + 1) * SPAN], out)
    return out


def softmax_rows(scores):
    weights = jnp.exp(scores - jnp.max(scores, axis=-1, keepdims=True))
    return weights / jnp.sum(weights, axis=-1, keepdims=True)


def probs_kernel(owners, q_ref, k_ref, out_ref):
    micro = pl.program_id(0)
    tokens, width = q_ref.shape[1], q_ref.shape[2]
    spans = tokens // SPAN
    for span in range(spans):
        refs = [owners[(micro * spans + span) * K_NBR + k] for k in range(K_NBR)]
        for pair in range(width // PAIR):
            cols = slice(pair * PAIR, (pair + 1) * PAIR)
            keys = jnp.concatenate([k_ref[r, :, cols] for r in refs], axis=0)
            rows = head_rows(q_ref[0, span * SPAN : (span + 1) * SPAN, cols])
            out_ref[0, span * (width // PAIR) + pair] = softmax_rows(nt(rows, keys) * SCALE).astype(BF)


def tick_kernel(
    chunks, base, head_major,
    scal,
    arriving, top, w_out, w_query, keys, values, probs, g0, s0, u0, d0,
    leaving, g_store, s_store, u_store, d_store,
    up, wo, wq, kb, vb, pb, datt, dq, gr, sem_up, sem_wo, sem_wq, sem_k, sem_v, sem_p, sem_out, sem_half, sem_head,
):
    micro = scal[base]
    valid = scal[base + 1]
    last = scal[base + 2]
    other = scal[base + 3]
    tokens, model = up.shape
    width = datt.shape[1]
    spans = tokens // SPAN
    refs = spans * K_NBR
    pairs = width // PAIR
    rows = model // chunks
    halves = sem_half.shape[0]
    block = model // (2 * halves)
    heads = sem_head.shape[0]
    slice_w = width // heads

    def copy_wo(c):
        return pltpu.make_async_copy(w_out.at[pl.ds(c * rows, rows)], wo.at[c], sem_wo.at[c])

    def copy_wq(c):
        return pltpu.make_async_copy(w_query.at[pl.ds(c * rows, rows)], wq.at[c], sem_wq.at[c])

    def copy_v(i):
        return pltpu.make_async_copy(values.at[scal[base + 4 + i]], vb.at[i], sem_v.at[i])

    def copy_k(i):
        return pltpu.make_async_copy(keys.at[scal[base + 4 + i]], kb.at[i], sem_k.at[i])

    @pl.when(valid > 0)
    def _():
        from_top = pltpu.make_async_copy(top.at[micro], up, sem_up)
        from_hop = pltpu.make_async_copy(arriving, up, sem_up)

        @pl.when(last > 0)
        def _():
            from_top.start()

        @pl.when(last == 0)
        def _():
            from_hop.start()

        for c in range(chunks):
            copy_wo(c).start()
        for i in range(refs):
            copy_v(i).start()
        get_probs = pltpu.make_async_copy(probs.at[micro], pb, sem_p)
        get_probs.start()
        for i in range(refs):
            copy_k(i).start()
        for c in range(chunks):
            copy_wq(c).start()

        from_hop.wait()
        saves = [pltpu.make_async_copy(up, u_store.at[micro], sem_out.at[0])]
        for h in range(halves):
            start = pl.multiple_of((2 * h + other) * block, block)
            saves.append(
                pltpu.make_async_copy(
                    up.at[:, pl.ds(start, block)],
                    s_store.at[micro, 1, :, pl.ds(h * block, block)],
                    sem_half.at[h],
                )
            )
        for save in saves:
            save.start()
        acc = None
        for c in range(chunks):
            copy_wo(c).wait()
            part = nn(up[:, c * rows : (c + 1) * rows], wo[c])
            acc = part if acc is None else acc + part
        datt[...] = acc.astype(BF)
        if head_major:
            late = [
                pltpu.make_async_copy(
                    datt.at[:, pl.ds(h * slice_w, slice_w)], d_store.at[h, micro], sem_head.at[h]
                )
                for h in range(heads)
            ]
        else:
            late = [pltpu.make_async_copy(datt, d_store.at[micro], sem_head.at[0])]
        for save in late:
            save.start()
        for i in range(refs):
            copy_v(i).wait()
        get_probs.wait()
        for i in range(refs):
            copy_k(i).wait()

        def one_span(span, carry):
            rws = pl.ds(pl.multiple_of(span * SPAN, SPAN), SPAN)
            for pair in range(pairs):
                cols = slice(pair * PAIR, (pair + 1) * PAIR)
                val = jnp.concatenate([vb[span * K_NBR + k, :, cols] for k in range(K_NBR)], axis=0)
                key = jnp.concatenate([kb[span * K_NBR + k, :, cols] for k in range(K_NBR)], axis=0)
                d_probs = nt(head_rows(datt[rws, cols]), val)
                prob = pb[span * pairs + pair].astype(F32)
                delta = jnp.sum(prob * d_probs, axis=-1, keepdims=True)
                d_scores = (prob * (d_probs - delta) * SCALE).astype(BF)
                dq[rws, cols] = head_columns(nn(d_scores, key)).astype(BF)
            return carry

        lax.fori_loop(0, spans, one_span, 0)
        late.append(pltpu.make_async_copy(dq, s_store.at[micro, 0], sem_out.at[1]))
        late[-1].start()
        for c in range(chunks):
            copy_wq(c).wait()
            cols = slice(c * rows, (c + 1) * rows)
            gr[:, cols] = (up[:, cols].astype(F32) + nt(dq[...], wq[c])).astype(BF)
        late.append(pltpu.make_async_copy(gr, leaving, sem_out.at[2]))
        late[-1].start()
        late.append(pltpu.make_async_copy(gr, g_store.at[micro], sem_out.at[3]))
        late[-1].start()
        for save in saves + late:
            save.wait()


def weight_grads_kernel(scale, par, x_own, x_got, up_own, dq_own, att_own, att_got, *parts_and_out):
    parts, out_ref = parts_and_out[:-1], parts_and_out[-1]
    flat, width = att_own.shape
    query_sum = tn(x_own[...], dq_own[...].reshape(flat, width))
    output_sum = tn(up_own[...], att_own[...])
    row = 0
    for dq_got, up_got in zip(parts[::2], parts[1::2]):
        count = dq_got.shape[0] * dq_got.shape[2]
        rws = slice(row, row + count)
        query_sum += tn(x_got[rws, :], dq_got[...].reshape(count, width))
        output_sum += tn(up_got[...].reshape(count, up_got.shape[-1]), att_got[rws, :])
        row += count
    out_ref[:, :width] = (query_sum * scale).astype(BF)
    out_ref[:, width:] = (output_sum * scale).astype(BF)


def attended_kernel(scal, values, probs, a0, a_store, vb, pb, att, sem_v, sem_p, sem_a):
    micros, tokens, width = a_store.shape
    spans = tokens // SPAN
    pairs = width // PAIR

    def get_probs(m):
        return pltpu.make_async_copy(probs.at[m], pb.at[m], sem_p.at[m])

    def put(m):
        return pltpu.make_async_copy(att.at[m], a_store.at[m], sem_a.at[m])

    @pl.when(scal[0] > 0)
    def _():
        get_values = pltpu.make_async_copy(values, vb, sem_v)
        get_values.start()
        for m in range(micros):
            get_probs(m).start()
        get_values.wait()

        def one(m, carry):
            get_probs(m).wait()
            for span in range(spans):
                rws = slice(span * SPAN, (span + 1) * SPAN)
                owners = [scal[1 + (m * spans + span) * K_NBR + k] for k in range(K_NBR)]
                for pair in range(pairs):
                    cols = slice(pair * PAIR, (pair + 1) * PAIR)
                    val = jnp.concatenate([vb[o, :, cols] for o in owners], axis=0)
                    att[m, rws, cols] = head_columns(nn(pb[m, span * pairs + pair], val)).astype(BF)
            put(m).start()
            return carry

        lax.fori_loop(0, micros, one, 0)
        for m in range(micros):
            put(m).wait()


def block_grads_kernel(micros, local, ids, mask, q_ref, d_ref, kv_ref, out_ref, acc):
    reader = pl.program_id(0)
    rows, width = d_ref.shape[1], d_ref.shape[2]
    tokens = rows // micros
    spans = tokens // SPAN
    readers = pl.num_programs(0)

    @pl.when(reader == 0)
    def _():
        acc[...] = jnp.zeros_like(acc)

    def block(r, which):
        start = pl.multiple_of((r % local * 2 + which) * NBR_LEN, NBR_LEN)
        return kv_ref[r // local, pl.ds(start, NBR_LEN), :]

    def unit(index, carry):
        at = [((index // spans * readers + reader) * spans + index % spans) * K_NBR + k for k in range(K_NBR)]
        rws = pl.ds(pl.multiple_of(index * SPAN, SPAN), SPAN)
        refs = [ids[i] for i in at]
        keep = [mask[i] > 0 for i in at]
        zero = jnp.zeros((NBR_LEN, width), BF)
        key = jnp.concatenate([jnp.where(m, block(r, 0), zero) for m, r in zip(keep, refs)], axis=0)
        val = jnp.concatenate([jnp.where(m, block(r, 1), zero) for m, r in zip(keep, refs)], axis=0)
        q_rows = head_rows(q_ref[0, rws, :])
        d_rows = head_rows(d_ref[0, rws, :])
        prob = softmax_rows(nt(q_rows, key) * SCALE)
        d_probs = nt(d_rows, val)
        delta = jnp.sum(prob * d_probs, axis=-1, keepdims=True)
        d_scores = (prob * (d_probs - delta) * SCALE).astype(BF)
        d_keys = tn(d_scores, q_rows)
        d_values = tn(prob.astype(BF), d_rows)
        fzero = jnp.zeros((NBR_LEN, width), F32)
        for k in range(K_NBR):
            part = slice(k * NBR_LEN, (k + 1) * NBR_LEN)
            acc[refs[k], 0] += jnp.where(keep[k], d_keys[part], fzero)
            acc[refs[k], 1] += jnp.where(keep[k], d_values[part], fzero)
        return carry

    lax.fori_loop(0, micros * spans, unit, 0, unroll=4)

    @pl.when(reader == readers - 1)
    def _():
        out_ref[...] = acc[...].astype(BF)


def body(
    section_inputs,
    top_grads,
    query_weight,
    output_weight,
    neighbour_kv,
    nbr_ids,
    send_list,
    send_counts,
):
    n_section = lax.axis_size("section")
    section_index = lax.axis_index("section")
    n_data = lax.axis_size("dp")
    data_index = lax.axis_index("dp")
    inputs_all = section_inputs[0]
    w_query = query_weight[0]
    w_out = output_weight[0]
    owned = neighbour_kv[0]
    micros, tokens, model = inputs_all.shape
    blk_dev = owned.shape[0]
    width = w_query.shape[1]
    spans = tokens // SPAN
    slice_w = width // n_data
    params = functools.partial(pltpu.CompilerParams, vmem_limit_bytes=56 << 20)

    my_list = lax.dynamic_index_in_dim(send_list, data_index, 0, keepdims=False)
    my_counts = lax.dynamic_index_in_dim(send_counts, data_index, 0, keepdims=False)

    def outbound(which):
        picked = jnp.zeros((n_data, NBR_LEN, width), BF)
        for b in range(blk_dev):
            chosen = ((my_list == b) & (my_counts > 0))[:, None, None]
            picked = jnp.where(chosen, owned[b, which][None], picked)
        return picked

    def exchange(x):
        return lax.all_to_all(x, "dp", split_axis=0, concat_axis=0, tiled=True)

    keys = exchange(outbound(0))
    values = exchange(outbound(1))
    query = nn(inputs_all.reshape(micros * tokens, model), w_query).astype(BF)
    query = query.reshape(micros, tokens, width)
    owners = (nbr_ids // blk_dev).astype(jnp.int32)

    probs = pl.pallas_call(
        probs_kernel,
        out_shape=jax.ShapeDtypeStruct((micros, spans * width // PAIR, 2 * SPAN, KEYS), BF),
        grid_spec=pltpu.PrefetchScalarGridSpec(
            num_scalar_prefetch=1,
            grid=(micros,),
            in_specs=[
                pl.BlockSpec((1, tokens, width), lambda i, o: (i, 0, 0)),
                pl.BlockSpec((n_data, NBR_LEN, width), lambda i, o: (0, 0, 0)),
            ],
            out_specs=pl.BlockSpec((1, spans * width // PAIR, 2 * SPAN, KEYS), lambda i, o: (i, 0, 0, 0)),
        ),
        compiler_params=params(),
    )(owners.reshape(-1), query, keys)

    def by_heads(x):
        return jnp.moveaxis(x.reshape(-1, n_data, slice_w), 1, 0)

    q_rows = micros * tokens
    kv_rows = blk_dev * 2 * NBR_LEN
    id_rows = micros * spans * K_NBR
    id_tile = jnp.broadcast_to(nbr_ids.reshape(1, id_rows, 1).astype(BF), (n_data, id_rows, slice_w))
    sliced = jnp.concatenate([by_heads(query), by_heads(owned), id_tile], axis=1)

    partners = [(i, i ^ 1) for i in range(n_data)]
    parity = data_index % 2
    flat = micros * tokens
    halves = n_data // 2
    half = model // 2
    block = model // n_data

    def swap(x):
        return lax.ppermute(x, "dp", partners)

    flat_in = inputs_all.reshape(flat, model)
    inputs_other = jnp.concatenate(
        [lax.dynamic_slice_in_dim(flat_in, (2 * h + 1 - parity) * block, block, axis=1) for h in range(halves)],
        axis=1,
    )

    chunks = 4
    ticks = micros + 2 * (n_section - 1)
    refs = spans * K_NBR
    micro_at = jnp.arange(ticks, dtype=jnp.int32) - 2 * (n_section - 1 - section_index)
    slot_at = jnp.clip(micro_at, 0, micros - 1)
    is_last = (section_index == n_section - 1).astype(jnp.int32)
    other = (1 - parity).astype(jnp.int32)
    table = jnp.concatenate(
        [
            slot_at[:, None],
            ((micro_at >= 0) & (micro_at < micros)).astype(jnp.int32)[:, None],
            jnp.broadcast_to(jnp.stack([is_last, other]), (ticks, 2)),
            jnp.take(owners.reshape(micros, refs), slot_at, axis=0),
        ],
        axis=1,
    ).astype(jnp.int32)
    scal = table.reshape(-1)
    head_major = slice_w % 128 == 0
    d_shape = (n_data, micros, tokens, slice_w) if head_major else (micros, tokens, width)
    store_shapes = (
        jax.ShapeDtypeStruct((micros, tokens, model), BF),
        jax.ShapeDtypeStruct((micros, 2, tokens, width), BF),
        jax.ShapeDtypeStruct((micros, tokens, model), BF),
        jax.ShapeDtypeStruct(d_shape, BF),
    )

    def tick(index, arriving, stores):
        return pl.pallas_call(
            functools.partial(tick_kernel, chunks, index * table.shape[1], head_major),
            out_shape=(jax.ShapeDtypeStruct((tokens, model), BF), *store_shapes),
            in_specs=[pl.BlockSpec(memory_space=pltpu.SMEM)] + [ANY] * 11,
            out_specs=[ANY] * 5,
            scratch_shapes=[
                pltpu.VMEM((tokens, model), BF),
                pltpu.VMEM((chunks, model // chunks, width), BF),
                pltpu.VMEM((chunks, model // chunks, width), BF),
                pltpu.VMEM((refs, NBR_LEN, width), BF),
                pltpu.VMEM((refs, NBR_LEN, width), BF),
                pltpu.VMEM((spans * width // PAIR, 2 * SPAN, KEYS), BF),
                pltpu.VMEM((tokens, width), BF),
                pltpu.VMEM((tokens, width), BF),
                pltpu.VMEM((tokens, model), BF),
                pltpu.SemaphoreType.DMA,
                pltpu.SemaphoreType.DMA((chunks,)),
                pltpu.SemaphoreType.DMA((chunks,)),
                pltpu.SemaphoreType.DMA((refs,)),
                pltpu.SemaphoreType.DMA((refs,)),
                pltpu.SemaphoreType.DMA,
                pltpu.SemaphoreType.DMA((4,)),
                pltpu.SemaphoreType.DMA((halves,)),
                pltpu.SemaphoreType.DMA((n_data if head_major else 1,)),
            ],
            input_output_aliases={8: 1, 9: 2, 10: 3, 11: 4},
            compiler_params=params(),
        )(scal, arriving, top_grads, w_out, w_query, keys, values, probs, *stores)

    def unwritten(*shapes):
        return pl.pallas_call(
            lambda *refs: None,
            out_shape=shapes,
            out_specs=[ANY] * len(shapes),
        )()

    def attend(enabled, store):
        return pl.pallas_call(
            attended_kernel,
            out_shape=jax.ShapeDtypeStruct((micros, tokens, width), BF),
            grid_spec=pltpu.PrefetchScalarGridSpec(
                num_scalar_prefetch=1,
                grid=(1,),
                in_specs=[ANY] * 3,
                out_specs=ANY,
                scratch_shapes=[
                    pltpu.VMEM((n_data, NBR_LEN, width), BF),
                    pltpu.VMEM((micros, spans * width // PAIR, 2 * SPAN, KEYS), BF),
                    pltpu.VMEM((micros, tokens, width), BF),
                    pltpu.SemaphoreType.DMA,
                    pltpu.SemaphoreType.DMA((micros,)),
                    pltpu.SemaphoreType.DMA((micros,)),
                ],
            ),
            input_output_aliases={3: 0},
            compiler_params=params(),
        )(jnp.concatenate([enabled[None].astype(jnp.int32), owners.reshape(-1)]), values, probs, store)

    *stores, attended = unwritten(*store_shapes, jax.ShapeDtypeStruct((micros, tokens, width), BF))
    attended = attend(1 - is_last, attended)
    arrived = [jnp.zeros((tokens, model), BF)] * 2
    got = []
    for index in range(ticks):
        leaving, *stores = tick(index, arrived[index], stores)
        if index == 0:
            sliced, inputs_other, leaving = lax.optimization_barrier((sliced, inputs_other, leaving))
            sliced = exchange(sliced)
            inputs_got = swap(inputs_other)
        hops = []
        for s in range(1, n_section):
            if 0 <= index - 2 * (n_section - 1 - s) < micros:
                hops.append((s, s - 1))
        arrived.append(lax.ppermute(leaving, "section", hops) if hops else leaving)
        if index == micros:
            attended = attend(is_last, attended)
            attended_got = swap(attended.reshape(flat, width))
        if index == ticks - 4:
            held = lax.optimization_barrier((arrived[index + 1], sliced, inputs_got))
            arrived[index + 1], sliced, inputs_got = held
        if index == ticks - 3:
            got.append(swap(stores[1][: micros - 2]))
        if index == ticks - 2:
            held = lax.optimization_barrier((arrived[index + 1], got[0], attended_got))
            arrived[index + 1], got[0], attended_got = held
    got.append(swap(stores[1][micros - 2 :]))
    grads_in, s_store, upstream, d_store = stores

    grad_scale = (flat * n_data) ** (-0.5)
    parts = []
    part_specs = []
    for part in got:
        count = part.shape[0]
        parts += [part, part]
        part_specs += [
            pl.BlockSpec((count, 1, tokens, width), lambda j, p: (0, 0, 0, 0)),
            pl.BlockSpec((count, 1, tokens, block), lambda j, p: (0, 1, 0, j)),
        ]
    terms = pl.pallas_call(
        functools.partial(weight_grads_kernel, grad_scale),
        out_shape=jax.ShapeDtypeStruct((half, 2 * width), BF),
        grid_spec=pltpu.PrefetchScalarGridSpec(
            num_scalar_prefetch=1,
            grid=(halves,),
            in_specs=[
                pl.BlockSpec((flat, block), lambda j, p: (0, 2 * j + p[0])),
                pl.BlockSpec((flat, block), lambda j, p: (0, j)),
                pl.BlockSpec((flat, block), lambda j, p: (0, 2 * j + p[0])),
                pl.BlockSpec((micros, 1, tokens, width), lambda j, p: (0, 0, 0, 0)),
                pl.BlockSpec((flat, width), lambda j, p: (0, 0)),
                pl.BlockSpec((flat, width), lambda j, p: (0, 0)),
                *part_specs,
            ],
            out_specs=pl.BlockSpec((block, 2 * width), lambda j, p: (j, 0)),
        ),
        compiler_params=params(),
    )(
        parity[None].astype(jnp.int32),
        inputs_all.reshape(flat, model),
        inputs_got,
        upstream.reshape(flat, model),
        s_store,
        attended.reshape(flat, width),
        attended_got,
        *parts,
    )
    d_heads = exchange(d_store) if head_major else exchange(by_heads(d_store))
    d_heads = d_heads.reshape(n_data, q_rows, slice_w)
    terms, d_heads = lax.optimization_barrier((terms, d_heads))
    shares = lax.psum_scatter(
        terms,
        "dp",
        scatter_dimension=0,
        tiled=True,
        axis_index_groups=[list(range(p, n_data, 2)) for p in range(2)],
    )

    ids_all = sliced[:, q_rows + kv_rows :, 0].astype(jnp.int32).reshape(n_data, micros, spans, K_NBR)
    ids_all = jnp.moveaxis(ids_all, 0, 1).reshape(micros, n_data * spans, K_NBR)
    owner_all = ids_all // blk_dev
    reader_all = (jnp.arange(n_data * spans, dtype=jnp.int32) // spans)[None, :, None]
    hit_owner = owner_all[..., None] == jnp.arange(n_data, dtype=jnp.int32)
    list_r = jnp.take(send_list, reader_all[0, :, 0], axis=1).T[None, :, None, :]
    count_r = jnp.take(send_counts, reader_all[0, :, 0], axis=1).T[None, :, None, :]
    block_all = owner_all * blk_dev + jnp.sum(jnp.where(hit_owner, list_r, 0), axis=-1)
    mask_all = jnp.sum(jnp.where(hit_owner, count_r, 0), axis=-1)
    blocks = n_data * blk_dev
    block_grads = pl.pallas_call(
        functools.partial(block_grads_kernel, micros, blk_dev),
        out_shape=jax.ShapeDtypeStruct((blocks, 2, NBR_LEN, slice_w), BF),
        grid_spec=pltpu.PrefetchScalarGridSpec(
            num_scalar_prefetch=2,
            grid=(n_data,),
            in_specs=[
                pl.BlockSpec((1, q_rows, slice_w), lambda i, a, b: (i, 0, 0)),
                pl.BlockSpec((1, q_rows, slice_w), lambda i, a, b: (i, 0, 0)),
                pl.BlockSpec((n_data, kv_rows, slice_w), lambda i, a, b: (0, q_rows // kv_rows, 0)),
            ],
            out_specs=pl.BlockSpec((blocks, 2, NBR_LEN, slice_w), lambda i, a, b: (0, 0, 0, 0)),
            scratch_shapes=[pltpu.VMEM((blocks, 2, NBR_LEN, slice_w), F32)],
        ),
        compiler_params=params(),
    )(block_all.reshape(-1).astype(jnp.int32), mask_all.reshape(-1).astype(jnp.int32), sliced, d_heads, sliced)
    returned = exchange(block_grads.reshape(n_data, blk_dev, 2, NBR_LEN, slice_w))
    kv_grads = jnp.moveaxis(returned, 0, -2).reshape(blk_dev, 2, NBR_LEN, width)
    return (
        grads_in[None],
        shares[None, :, :width],
        shares[None, :, width:],
        kv_grads[None],
    )


def solution(mesh):
    in_specs = (
        P("section", None, "dp", None),
        P(None, "dp", None),
        P("section", None, None),
        P("section", None, None),
        P("section", "dp", None, None, None),
        P(None, "dp", None),
        P(),
        P(),
    )
    out_specs = (
        P("section", None, "dp", None),
        P("section", "dp", None),
        P("section", "dp", None),
        P("section", "dp", None, None, None),
    )
    return jax.shard_map(body, mesh=mesh, in_specs=in_specs, out_specs=out_specs, check_vma=False)
```

```python
import functools

import jax
import jax.numpy as jnp
from jax import lax
from jax.experimental import pallas as pl
from jax.experimental.pallas import tpu as pltpu
from jax.sharding import PartitionSpec as P

HEADS = 16
HEAD_DIM = 64
SPAN = 64
K_NBR = 2
NBR_LEN = 128
PAIR = 2 * HEAD_DIM
KEYS = K_NBR * NBR_LEN
SCALE = HEAD_DIM ** (-0.5)
BF = jnp.bfloat16
F32 = jnp.float32
ANY = pl.BlockSpec(memory_space=pl.ANY)


def cost(micros_of_work):
    return pl.CostEstimate(flops=0, transcendentals=0, bytes_accessed=int(micros_of_work * 3.6e6))


def nt(a, b):
    return lax.dot_general(a, b, (((1,), (1,)), ((), ())), preferred_element_type=F32)


def nn(a, b):
    return lax.dot_general(a, b, (((1,), (0,)), ((), ())), preferred_element_type=F32)


def tn(a, b):
    return lax.dot_general(a, b, (((0,), (0,)), ((), ())), preferred_element_type=F32)


def head_rows(x):
    heads = x.shape[1] // HEAD_DIM
    if heads == 1:
        return x
    lane = lax.broadcasted_iota(jnp.int32, x.shape, 1) // HEAD_DIM
    zero = jnp.zeros_like(x)
    return jnp.concatenate([jnp.where(lane == h, x, zero) for h in range(heads)], axis=0)


def head_columns(y):
    heads = y.shape[1] // HEAD_DIM
    out = y[:SPAN]
    lane = lax.broadcasted_iota(jnp.int32, out.shape, 1) // HEAD_DIM
    for h in range(1, heads):
        out = jnp.where(lane == h, y[h * SPAN : (h + 1) * SPAN], out)
    return out


def softmax_rows(scores):
    weights = jnp.exp(scores - jnp.max(scores, axis=-1, keepdims=True))
    return weights / jnp.sum(weights, axis=-1, keepdims=True)


def probs_kernel(owners, q_ref, k_ref, out_ref):
    micro = pl.program_id(0)
    tokens, width = q_ref.shape[1], q_ref.shape[2]
    spans = tokens // SPAN
    for span in range(spans):
        refs = [owners[(micro * spans + span) * K_NBR + k] for k in range(K_NBR)]
        for pair in range(width // PAIR):
            cols = slice(pair * PAIR, (pair + 1) * PAIR)
            keys = jnp.concatenate([k_ref[r, :, cols] for r in refs], axis=0)
            rows = head_rows(q_ref[0, span * SPAN : (span + 1) * SPAN, cols])
            out_ref[0, span * (width // PAIR) + pair] = softmax_rows(nt(rows, keys) * SCALE).astype(BF)


def tick_kernel(
    chunks, base, head_major,
    scal,
    arriving, top, w_out, w_query, keys, values, probs, g0, u0, d0, sb0, sa0,
    leaving, g_store, u_store, d_store, s_late, s_early,
    up, wo, wq, kb, vb, pb, datt, dq, gr, sem_up, sem_wo, sem_wq, sem_k, sem_v, sem_p, sem_out, sem_half, sem_head,
):
    micro = scal[base]
    valid = scal[base + 1]
    last = scal[base + 2]
    other = scal[base + 3]
    tokens, model = up.shape
    width = datt.shape[1]
    spans = tokens // SPAN
    refs = spans * K_NBR
    pairs = width // PAIR
    rows = model // chunks
    wide = width // chunks
    groups = 1
    halves = sem_half.shape[0]
    block = model // (2 * halves)
    heads = sem_head.shape[0]
    slice_w = width // heads

    def copy_wo(c):
        return pltpu.make_async_copy(w_out.at[:, pl.ds(c * wide, wide)], wo.at[c], sem_wo.at[c])

    def copy_wq(c):
        return pltpu.make_async_copy(w_query.at[pl.ds(c * rows, rows)], wq.at[c], sem_wq.at[c])

    def copy_v(i):
        return pltpu.make_async_copy(values.at[scal[base + 4 + i]], vb.at[i], sem_v.at[i])

    def copy_k(i):
        return pltpu.make_async_copy(keys.at[scal[base + 4 + i]], kb.at[i], sem_k.at[i])

    @pl.when(valid > 0)
    def _():
        from_top = pltpu.make_async_copy(top.at[micro], up, sem_up)
        from_hop = pltpu.make_async_copy(arriving, up, sem_up)

        @pl.when(last > 0)
        def _():
            from_top.start()

        @pl.when(last == 0)
        def _():
            from_hop.start()

        for c in range(chunks):
            copy_wo(c).start()
        for i in range(refs):
            copy_v(i).start()
        get_probs = pltpu.make_async_copy(probs.at[micro], pb, sem_p)
        get_probs.start()
        for i in range(refs):
            copy_k(i).start()
        for c in range(chunks):
            copy_wq(c).start()

        from_hop.wait()
        save_up = pltpu.make_async_copy(up, u_store.at[micro], sem_out.at[0])
        save_up.start()
        cut = s_early.shape[0]

        def to_swap(late):
            store = s_late.at[micro - cut] if late else s_early.at[micro]
            copies = [pltpu.make_async_copy(dq, store.at[0], sem_out.at[1])]
            for h in range(halves):
                start = pl.multiple_of((2 * h + other) * block, block)
                copies.append(
                    pltpu.make_async_copy(
                        up.at[:, pl.ds(start, block)], store.at[1, :, pl.ds(h * block, block)], sem_half.at[h]
                    )
                )
            return copies

        @pl.when(micro < cut)
        def _():
            for copy in to_swap(False)[1:]:
                copy.start()

        @pl.when(micro >= cut)
        def _():
            for copy in to_swap(True)[1:]:
                copy.start()


        def project(c, carry):
            copy_wo(c).wait()
            datt[:, pl.ds(pl.multiple_of(c * wide, wide), wide)] = nn(up[...], wo[c]).astype(BF)
            return carry

        lax.fori_loop(0, chunks, project, 0)
        if head_major:
            late = [
                pltpu.make_async_copy(
                    datt.at[:, pl.ds(h * slice_w, slice_w)], d_store.at[h, micro], sem_head.at[h]
                )
                for h in range(heads)
            ]
        else:
            late = [pltpu.make_async_copy(datt, d_store.at[micro], sem_head.at[0])]
        for save in late:
            save.start()
        for i in range(refs):
            copy_v(i).wait()
        get_probs.wait()
        for i in range(refs):
            copy_k(i).wait()

        def one_group(index, carry):
            span, first = index // groups, index % groups * (pairs // groups)
            rws = pl.ds(pl.multiple_of(span * SPAN, SPAN), SPAN)
            for step in range(pairs // groups):
                pair = first + step
                cols = pl.ds(pl.multiple_of(pair * PAIR, PAIR), PAIR)
                val = jnp.concatenate([vb[span * K_NBR + k, :, cols] for k in range(K_NBR)], axis=0)
                key = jnp.concatenate([kb[span * K_NBR + k, :, cols] for k in range(K_NBR)], axis=0)
                d_probs = nt(head_rows(datt[rws, cols]), val)
                prob = pb[span * pairs + pair].astype(F32)
                delta = jnp.sum(prob * d_probs, axis=-1, keepdims=True)
                d_scores = (prob * (d_probs - delta) * SCALE).astype(BF)
                dq[rws, cols] = head_columns(nn(d_scores, key)).astype(BF)
            return carry

        lax.fori_loop(0, spans * groups, one_group, 0)

        @pl.when(micro < cut)
        def _():
            to_swap(False)[0].start()

        @pl.when(micro >= cut)
        def _():
            to_swap(True)[0].start()

        def back(c, carry):
            copy_wq(c).wait()
            cols = pl.ds(pl.multiple_of(c * rows, rows), rows)
            gr[:, cols] = (up[:, cols].astype(F32) + nt(dq[...], wq[c])).astype(BF)
            return carry

        lax.fori_loop(0, chunks, back, 0)
        late.append(pltpu.make_async_copy(gr, leaving, sem_out.at[2]))
        late[-1].start()
        late.append(pltpu.make_async_copy(gr, g_store.at[micro], sem_out.at[3]))
        late[-1].start()
        for save in [save_up] + late:
            save.wait()

        @pl.when(micro < cut)
        def _():
            for copy in to_swap(False):
                copy.wait()

        @pl.when(micro >= cut)
        def _():
            for copy in to_swap(True):
                copy.wait()


def weight_grads_kernel(scale, par, x_own, x_got, up_own, att_own, att_got, *parts_and_out):
    parts, out_ref = parts_and_out[:-1], parts_and_out[-1]
    flat, width = att_own.shape
    output_sum = tn(up_own[...], att_own[...])
    query_sum = 0.0
    row = 0
    for dq_own, dq_got, up_got in zip(parts[::3], parts[1::3], parts[2::3]):
        count = dq_got.shape[0] * dq_got.shape[2]
        rws = slice(row, row + count)
        query_sum += tn(x_own[rws, :], dq_own[...].reshape(count, width))
        query_sum += tn(x_got[rws, :], dq_got[...].reshape(count, width))
        output_sum += tn(up_got[...].reshape(count, up_got.shape[-1]), att_got[rws, :])
        row += count
    out_ref[:, :width] = (query_sum * scale).astype(BF)
    out_ref[:, width:] = (output_sum * scale).astype(BF)


def attended_kernel(scal, values, probs, a0, a_store, vb, pb, att, sem_v, sem_p, sem_a):
    micros, tokens, width = a_store.shape
    spans = tokens // SPAN
    pairs = width // PAIR

    def get_probs(m):
        return pltpu.make_async_copy(probs.at[m], pb.at[m], sem_p.at[m])

    def put(m):
        return pltpu.make_async_copy(att.at[m], a_store.at[m], sem_a.at[m])

    @pl.when(scal[0] > 0)
    def _():
        get_values = pltpu.make_async_copy(values, vb, sem_v)
        get_values.start()
        for m in range(micros):
            get_probs(m).start()
        get_values.wait()

        def one(m, carry):
            get_probs(m).wait()
            for span in range(spans):
                rws = slice(span * SPAN, (span + 1) * SPAN)
                owners = [scal[1 + (m * spans + span) * K_NBR + k] for k in range(K_NBR)]
                for pair in range(pairs):
                    cols = slice(pair * PAIR, (pair + 1) * PAIR)
                    val = jnp.concatenate([vb[o, :, cols] for o in owners], axis=0)
                    att[m, rws, cols] = head_columns(nn(pb[m, span * pairs + pair], val)).astype(BF)
            put(m).start()
            return carry

        lax.fori_loop(0, micros, one, 0)
        for m in range(micros):
            put(m).wait()


def block_grads_kernel(micros, local, ids, mask, q_ref, d_ref, kv_ref, out_ref, acc):
    reader = pl.program_id(0)
    rows, width = d_ref.shape[1], d_ref.shape[2]
    tokens = rows // micros
    spans = tokens // SPAN
    readers = pl.num_programs(0)

    @pl.when(reader == 0)
    def _():
        acc[...] = jnp.zeros_like(acc)

    def block(r, which):
        start = pl.multiple_of((r % local * 2 + which) * NBR_LEN, NBR_LEN)
        return kv_ref[r // local, pl.ds(start, NBR_LEN), :]

    def unit(index, carry):
        at = [((index // spans * readers + reader) * spans + index % spans) * K_NBR + k for k in range(K_NBR)]
        rws = pl.ds(pl.multiple_of(index * SPAN, SPAN), SPAN)
        refs = [ids[i] for i in at]
        keep = [mask[i] > 0 for i in at]
        zero = jnp.zeros((NBR_LEN, width), BF)
        key = jnp.concatenate([jnp.where(m, block(r, 0), zero) for m, r in zip(keep, refs)], axis=0)
        val = jnp.concatenate([jnp.where(m, block(r, 1), zero) for m, r in zip(keep, refs)], axis=0)
        q_rows = head_rows(q_ref[0, rws, :])
        d_rows = head_rows(d_ref[0, rws, :])
        scores = nt(key, q_rows) * SCALE
        weights = jnp.exp(scores - jnp.max(scores, axis=0, keepdims=True))
        prob = weights / jnp.sum(weights, axis=0, keepdims=True)
        d_probs = nt(val, d_rows)
        delta = jnp.sum(prob * d_probs, axis=0, keepdims=True)
        d_scores = (prob * (d_probs - delta) * SCALE).astype(BF)
        d_keys = nn(d_scores, q_rows)
        d_values = nn(prob.astype(BF), d_rows)
        fzero = jnp.zeros((NBR_LEN, width), F32)
        for k in range(K_NBR):
            part = slice(k * NBR_LEN, (k + 1) * NBR_LEN)
            acc[refs[k], 0] += jnp.where(keep[k], d_keys[part], fzero)
            acc[refs[k], 1] += jnp.where(keep[k], d_values[part], fzero)
        return carry

    lax.fori_loop(0, micros * spans, unit, 0, unroll=4)

    @pl.when(reader == readers - 1)
    def _():
        out_ref[...] = acc[...].astype(BF)


def body(
    section_inputs,
    top_grads,
    query_weight,
    output_weight,
    neighbour_kv,
    nbr_ids,
    send_list,
    send_counts,
):
    n_section = lax.axis_size("section")
    section_index = lax.axis_index("section")
    n_data = lax.axis_size("dp")
    data_index = lax.axis_index("dp")
    inputs_all = section_inputs[0]
    w_query = query_weight[0]
    w_out = output_weight[0]
    owned = neighbour_kv[0]
    micros, tokens, model = inputs_all.shape
    blk_dev = owned.shape[0]
    width = w_query.shape[1]
    spans = tokens // SPAN
    slice_w = width // n_data
    params = functools.partial(pltpu.CompilerParams, vmem_limit_bytes=56 << 20)

    near = n_data // 2
    mates = data_index ^ jnp.arange(near, dtype=jnp.int32)

    def wanted(owner):
        row = lax.dynamic_index_in_dim(send_list, owner, 0, keepdims=False)
        counts = lax.dynamic_index_in_dim(send_counts, owner, 0, keepdims=False)
        return jnp.take(row, mates), jnp.take(counts, mates)

    wants = [wanted(data_index), wanted(data_index ^ near)]

    def across(which, behind):
        own = owned[:, which]
        if behind is not None:
            own, behind = lax.optimization_barrier((own, behind))
        return own, lax.ppermute(own, "dp", [(i, i ^ near) for i in range(n_data)])

    def picked(copies):
        pieces = []
        for k in range(near):
            piece = []
            for blocks, (which_block, counts) in zip(copies, wants):
                chosen = jnp.zeros((NBR_LEN, width), BF)
                for b in range(blk_dev):
                    chosen = jnp.where((which_block[k] == b) & (counts[k] > 0), blocks[b], chosen)
                piece.append(chosen)
            pieces.append(jnp.stack(piece))
        return pieces

    def fetch(pieces):
        moved = [lax.ppermute(pieces[k], "dp", [(i, i ^ k) for i in range(n_data)]) for k in range(1, near)]
        return jnp.concatenate(pieces[:1] + moved, axis=0)

    def exchange(x):
        return lax.all_to_all(x, "dp", split_axis=0, concat_axis=0, tiled=True)

    key_copies = across(0, None)
    value_copies = across(1, key_copies[1])
    key_pieces, inputs_all = lax.optimization_barrier((picked(key_copies), inputs_all))
    keys = fetch(key_pieces)
    query = nn(inputs_all.reshape(micros * tokens, model), w_query).astype(BF)
    held = lax.optimization_barrier((picked(value_copies), query, inputs_all, owned, nbr_ids))
    value_pieces, query, inputs_all, owned, nbr_ids = held
    values = fetch(value_pieces)
    query = query.reshape(micros, tokens, width)
    apart = (nbr_ids // blk_dev).astype(jnp.int32) ^ data_index
    owners = apart % near * 2 + apart // near

    probs = pl.pallas_call(
        probs_kernel,
        cost_estimate=cost(7),
        out_shape=jax.ShapeDtypeStruct((micros, spans * width // PAIR, 2 * SPAN, KEYS), BF),
        grid_spec=pltpu.PrefetchScalarGridSpec(
            num_scalar_prefetch=1,
            grid=(micros,),
            in_specs=[
                pl.BlockSpec((1, tokens, width), lambda i, o: (i, 0, 0)),
                pl.BlockSpec((n_data, NBR_LEN, width), lambda i, o: (0, 0, 0)),
            ],
            out_specs=pl.BlockSpec((1, spans * width // PAIR, 2 * SPAN, KEYS), lambda i, o: (i, 0, 0, 0)),
        ),
        compiler_params=params(),
    )(owners.reshape(-1), query, keys)

    def by_heads(x):
        return jnp.moveaxis(x.reshape(-1, n_data, slice_w), 1, 0)

    q_rows = micros * tokens
    kv_rows = blk_dev * 2 * NBR_LEN
    id_rows = micros * spans * K_NBR
    id_tile = jnp.broadcast_to(nbr_ids.reshape(1, id_rows, 1).astype(BF), (n_data, id_rows, slice_w))
    sliced = jnp.concatenate([by_heads(query), by_heads(owned), id_tile], axis=1)

    partners = [(i, i ^ 1) for i in range(n_data)]
    parity = data_index % 2
    flat = micros * tokens
    halves = n_data // 2
    half = model // 2
    block = model // n_data

    def swap(x):
        return lax.ppermute(x, "dp", partners)

    flat_in = inputs_all.reshape(flat, model)
    inputs_other = jnp.concatenate(
        [lax.dynamic_slice_in_dim(flat_in, (2 * h + 1 - parity) * block, block, axis=1) for h in range(halves)],
        axis=1,
    )

    chunks = 4
    ticks = micros + 2 * (n_section - 1)
    refs = spans * K_NBR
    micro_at = jnp.arange(ticks, dtype=jnp.int32) - 2 * (n_section - 1 - section_index)
    slot_at = jnp.clip(micro_at, 0, micros - 1)
    is_last = (section_index == n_section - 1).astype(jnp.int32)
    other = (1 - parity).astype(jnp.int32)
    table = jnp.concatenate(
        [
            slot_at[:, None],
            ((micro_at >= 0) & (micro_at < micros)).astype(jnp.int32)[:, None],
            jnp.broadcast_to(jnp.stack([is_last, other]), (ticks, 2)),
            jnp.take(owners.reshape(micros, refs), slot_at, axis=0),
        ],
        axis=1,
    ).astype(jnp.int32)
    scal = table.reshape(-1)
    head_major = slice_w % 128 == 0
    d_shape = (n_data, micros, tokens, slice_w) if head_major else (micros, tokens, width)
    cut = micros // 2
    store_shapes = (
        jax.ShapeDtypeStruct((micros, tokens, model), BF),
        jax.ShapeDtypeStruct((micros, tokens, model), BF),
        jax.ShapeDtypeStruct(d_shape, BF),
        jax.ShapeDtypeStruct((micros - cut, 2, tokens, width), BF),
        jax.ShapeDtypeStruct((cut, 2, tokens, width), BF),
    )

    def tick(index, arriving, stores):
        return pl.pallas_call(
            functools.partial(tick_kernel, chunks, index * table.shape[1], head_major),
            out_shape=(jax.ShapeDtypeStruct((tokens, model), BF), *store_shapes),
            in_specs=[pl.BlockSpec(memory_space=pltpu.SMEM)] + [ANY] * 12,
            out_specs=[ANY] * 6,
            scratch_shapes=[
                pltpu.VMEM((tokens, model), BF),
                pltpu.VMEM((chunks, model, width // chunks), BF),
                pltpu.VMEM((chunks, model // chunks, width), BF),
                pltpu.VMEM((refs, NBR_LEN, width), BF),
                pltpu.VMEM((refs, NBR_LEN, width), BF),
                pltpu.VMEM((spans * width // PAIR, 2 * SPAN, KEYS), BF),
                pltpu.VMEM((tokens, width), BF),
                pltpu.VMEM((tokens, width), BF),
                pltpu.VMEM((tokens, model), BF),
                pltpu.SemaphoreType.DMA,
                pltpu.SemaphoreType.DMA((chunks,)),
                pltpu.SemaphoreType.DMA((chunks,)),
                pltpu.SemaphoreType.DMA((refs,)),
                pltpu.SemaphoreType.DMA((refs,)),
                pltpu.SemaphoreType.DMA,
                pltpu.SemaphoreType.DMA((4,)),
                pltpu.SemaphoreType.DMA((halves,)),
                pltpu.SemaphoreType.DMA((n_data if head_major else 1,)),
            ],
            input_output_aliases={8: 1, 9: 2, 10: 3, 11: 4, 12: 5},
            cost_estimate=cost(11),
            compiler_params=params(),
        )(scal, arriving, top_grads, w_out, w_query, keys, values, probs, *stores)

    def unwritten(*shapes):
        return pl.pallas_call(
            lambda *refs: None,
            out_shape=shapes,
            out_specs=[ANY] * len(shapes),
        )()

    def attend(enabled, store):
        return pl.pallas_call(
            attended_kernel,
            out_shape=jax.ShapeDtypeStruct((micros, tokens, width), BF),
            grid_spec=pltpu.PrefetchScalarGridSpec(
                num_scalar_prefetch=1,
                grid=(1,),
                in_specs=[ANY] * 3,
                out_specs=ANY,
                scratch_shapes=[
                    pltpu.VMEM((n_data, NBR_LEN, width), BF),
                    pltpu.VMEM((micros, spans * width // PAIR, 2 * SPAN, KEYS), BF),
                    pltpu.VMEM((micros, tokens, width), BF),
                    pltpu.SemaphoreType.DMA,
                    pltpu.SemaphoreType.DMA((micros,)),
                    pltpu.SemaphoreType.DMA((micros,)),
                ],
            ),
            input_output_aliases={3: 0},
            cost_estimate=cost(5),
            compiler_params=params(),
        )(jnp.concatenate([enabled[None].astype(jnp.int32), owners.reshape(-1)]), values, probs, store)

    *stores, attended = unwritten(*store_shapes, jax.ShapeDtypeStruct((micros, tokens, width), BF))
    arrived = [jnp.zeros((tokens, model), BF)] * 2
    got = []
    for index in range(ticks):
        if index == micros + 3:
            arrived[index], attended_got = lax.optimization_barrier((arrived[index], attended_got))
        leaving, *stores = tick(index, arrived[index], stores)
        if index == 0:
            sliced, inputs_other, leaving, attended = lax.optimization_barrier((sliced, inputs_other, leaving, attended))
            sliced = exchange(sliced)
            inputs_got = swap(inputs_other)
            attended = attend(1 - is_last, attended)
            stores[0], attended = lax.optimization_barrier((stores[0], attended))
        hops = []
        for s in range(1, n_section):
            if 0 <= index - 2 * (n_section - 1 - s) < micros:
                hops.append((s, s - 1))
        if index > 0:
            held = lax.optimization_barrier((leaving, arrived[index + 1]))
            if hops:
                leaving, arrived[index + 1] = held
        arrived.append(lax.ppermute(leaving, "section", hops) if hops else leaving)
        if index == micros:
            attended = attend(is_last, attended)
            stores[0], attended = lax.optimization_barrier((stores[0], attended))
            held = lax.optimization_barrier((arrived[index + 1], sliced, inputs_got))
            arrived[index + 1], sliced, inputs_got = held
            attended_got = swap(attended.reshape(flat, width))
        if index == ticks - micros + cut - 1:
            stores[4], arrived[index + 1] = lax.optimization_barrier((stores[4], arrived[index + 1]))
            got.append(swap(stores[4]))
    grads_in, upstream, d_store, s_late, s_early = stores
    got[0], s_late, d_store = lax.optimization_barrier((got[0], s_late, d_store))
    got.append(swap(s_late))
    grad_scale = (flat * n_data) ** (-0.5)
    parts = []
    part_specs = []
    for own, part in zip((s_early, s_late), got):
        count = part.shape[0]
        parts += [own, part, part]
        part_specs += [
            pl.BlockSpec((count, 1, tokens, width), lambda j, p: (0, 0, 0, 0)),
            pl.BlockSpec((count, 1, tokens, width), lambda j, p: (0, 0, 0, 0)),
            pl.BlockSpec((count, 1, tokens, block), lambda j, p: (0, 1, 0, j)),
        ]
    terms = pl.pallas_call(
        functools.partial(weight_grads_kernel, grad_scale),
        cost_estimate=cost(9),
        out_shape=jax.ShapeDtypeStruct((half, 2 * width), BF),
        grid_spec=pltpu.PrefetchScalarGridSpec(
            num_scalar_prefetch=1,
            grid=(halves,),
            in_specs=[
                pl.BlockSpec((flat, block), lambda j, p: (0, 2 * j + p[0])),
                pl.BlockSpec((flat, block), lambda j, p: (0, j)),
                pl.BlockSpec((flat, block), lambda j, p: (0, 2 * j + p[0])),
                pl.BlockSpec((flat, width), lambda j, p: (0, 0)),
                pl.BlockSpec((flat, width), lambda j, p: (0, 0)),
                *part_specs,
            ],
            out_specs=pl.BlockSpec((block, 2 * width), lambda j, p: (j, 0)),
        ),
        compiler_params=params(),
    )(
        parity[None].astype(jnp.int32),
        inputs_all.reshape(flat, model),
        inputs_got,
        upstream.reshape(flat, model),
        attended.reshape(flat, width),
        attended_got,
        *parts,
    )
    d_heads = exchange(d_store) if head_major else exchange(by_heads(d_store))
    d_heads = d_heads.reshape(n_data, q_rows, slice_w)
    terms, d_heads = lax.optimization_barrier((terms, d_heads))
    shares = lax.psum_scatter(
        terms,
        "dp",
        scatter_dimension=0,
        tiled=True,
        axis_index_groups=[list(range(p, n_data, 2)) for p in range(2)],
    )

    ids_all = sliced[:, q_rows + kv_rows :, 0].astype(jnp.int32).reshape(n_data, micros, spans, K_NBR)
    ids_all = jnp.moveaxis(ids_all, 0, 1).reshape(micros, n_data * spans, K_NBR)
    owner_all = ids_all // blk_dev
    reader_all = (jnp.arange(n_data * spans, dtype=jnp.int32) // spans)[None, :, None]
    hit_owner = owner_all[..., None] == jnp.arange(n_data, dtype=jnp.int32)
    list_r = jnp.take(send_list, reader_all[0, :, 0], axis=1).T[None, :, None, :]
    count_r = jnp.take(send_counts, reader_all[0, :, 0], axis=1).T[None, :, None, :]
    block_all = owner_all * blk_dev + jnp.sum(jnp.where(hit_owner, list_r, 0), axis=-1)
    mask_all = jnp.sum(jnp.where(hit_owner, count_r, 0), axis=-1)
    blocks = n_data * blk_dev
    block_grads = pl.pallas_call(
        functools.partial(block_grads_kernel, micros, blk_dev),
        cost_estimate=cost(37),
        out_shape=jax.ShapeDtypeStruct((blocks, 2, NBR_LEN, slice_w), BF),
        grid_spec=pltpu.PrefetchScalarGridSpec(
            num_scalar_prefetch=2,
            grid=(n_data,),
            in_specs=[
                pl.BlockSpec((1, q_rows, slice_w), lambda i, a, b: (i, 0, 0)),
                pl.BlockSpec((1, q_rows, slice_w), lambda i, a, b: (i, 0, 0)),
                pl.BlockSpec((n_data, kv_rows, slice_w), lambda i, a, b: (0, q_rows // kv_rows, 0)),
            ],
            out_specs=pl.BlockSpec((blocks, 2, NBR_LEN, slice_w), lambda i, a, b: (0, 0, 0, 0)),
            scratch_shapes=[pltpu.VMEM((blocks, 2, NBR_LEN, slice_w), F32)],
        ),
        compiler_params=params(),
    )(block_all.reshape(-1).astype(jnp.int32), mask_all.reshape(-1).astype(jnp.int32), sliced, d_heads, sliced)
    returned = exchange(block_grads.reshape(n_data, blk_dev, 2, NBR_LEN, slice_w))
    kv_grads = jnp.moveaxis(returned, 0, -2).reshape(blk_dev, 2, NBR_LEN, width)
    return (
        grads_in[None],
        shares[None, :, :width],
        shares[None, :, width:],
        kv_grads[None],
    )


def solution(mesh):
    in_specs = (
        P("section", None, "dp", None),
        P(None, "dp", None),
        P("section", None, None),
        P("section", None, None),
        P("section", "dp", None, None, None),
        P(None, "dp", None),
        P(),
        P(),
    )
    out_specs = (
        P("section", None, "dp", None),
        P("section", "dp", None),
        P("section", "dp", None),
        P("section", "dp", None, None, None),
    )
    return jax.shard_map(body, mesh=mesh, in_specs=in_specs, out_specs=out_specs, check_vma=False)
```

```python
import functools

import jax
import jax.numpy as jnp
from jax import lax
from jax.experimental import pallas as pl
from jax.experimental.pallas import tpu as pltpu
from jax.sharding import PartitionSpec as P

HEADS = 16
HEAD_DIM = 64
SPAN = 64
K_NBR = 2
NBR_LEN = 128
PAIR = 2 * HEAD_DIM
KEYS = K_NBR * NBR_LEN
SCALE = HEAD_DIM ** (-0.5)
BF = jnp.bfloat16
F32 = jnp.float32
ANY = pl.BlockSpec(memory_space=pl.ANY)


def cost(micros_of_work):
    return pl.CostEstimate(flops=0, transcendentals=0, bytes_accessed=int(micros_of_work * 3.6e6))


def nt(a, b):
    return lax.dot_general(a, b, (((1,), (1,)), ((), ())), preferred_element_type=F32)


def nn(a, b):
    return lax.dot_general(a, b, (((1,), (0,)), ((), ())), preferred_element_type=F32)


def tn(a, b):
    return lax.dot_general(a, b, (((0,), (0,)), ((), ())), preferred_element_type=F32)


def head_rows(x):
    heads = x.shape[1] // HEAD_DIM
    if heads == 1:
        return x
    lane = lax.broadcasted_iota(jnp.int32, x.shape, 1) // HEAD_DIM
    zero = jnp.zeros_like(x)
    return jnp.concatenate([jnp.where(lane == h, x, zero) for h in range(heads)], axis=0)


def head_columns(y):
    heads = y.shape[1] // HEAD_DIM
    out = y[:SPAN]
    lane = lax.broadcasted_iota(jnp.int32, out.shape, 1) // HEAD_DIM
    for h in range(1, heads):
        out = jnp.where(lane == h, y[h * SPAN : (h + 1) * SPAN], out)
    return out


def softmax_rows(scores):
    weights = jnp.exp(scores - jnp.max(scores, axis=-1, keepdims=True))
    return weights / jnp.sum(weights, axis=-1, keepdims=True)


def probs_kernel(owners, q_ref, k_ref, out_ref):
    micro = pl.program_id(0)
    tokens, width = q_ref.shape[1], q_ref.shape[2]
    spans = tokens // SPAN
    for span in range(spans):
        refs = [owners[(micro * spans + span) * K_NBR + k] for k in range(K_NBR)]
        for pair in range(width // PAIR):
            cols = slice(pair * PAIR, (pair + 1) * PAIR)
            keys = jnp.concatenate([k_ref[r, :, cols] for r in refs], axis=0)
            rows = head_rows(q_ref[0, span * SPAN : (span + 1) * SPAN, cols])
            out_ref[0, span * (width // PAIR) + pair] = softmax_rows(nt(rows, keys) * SCALE).astype(BF)


def tick_kernel(
    chunks, base, head_major, live,
    scal,
    arriving, top, w_out, w_query, keys, values, probs,
    *refs,
):
    count = 3 + len(live)
    leaving, g_store, u_store, d_store, *s_stores = refs[count : 2 * count + 1]
    (
        up, wo, wq, kb, vb, pb, datt, dq, gr,
        sem_up, sem_wo, sem_wq, sem_k, sem_v, sem_p, sem_out, sem_half, sem_head,
    ) = refs[2 * count + 1 :]
    micro = scal[base]
    valid = scal[base + 1]
    last = scal[base + 2]
    other = scal[base + 3]
    tokens, model = up.shape
    width = datt.shape[1]
    spans = tokens // SPAN
    span_refs = spans * K_NBR
    pairs = width // PAIR
    rows = model // chunks
    wide = width // chunks
    groups = 1
    halves = sem_half.shape[0]
    block = model // (2 * halves)
    heads = sem_head.shape[0]
    slice_w = width // heads

    def copy_wo(c):
        return pltpu.make_async_copy(w_out.at[:, pl.ds(c * wide, wide)], wo.at[c], sem_wo.at[c])

    def copy_wq(c):
        return pltpu.make_async_copy(w_query.at[pl.ds(c * rows, rows)], wq.at[c], sem_wq.at[c])

    def copy_v(i):
        return pltpu.make_async_copy(values.at[scal[base + 4 + i]], vb.at[i], sem_v.at[i])

    def copy_k(i):
        return pltpu.make_async_copy(keys.at[scal[base + 4 + i]], kb.at[i], sem_k.at[i])

    @pl.when(valid > 0)
    def _():
        from_top = pltpu.make_async_copy(top.at[micro], up, sem_up)
        from_hop = pltpu.make_async_copy(arriving, up, sem_up)

        @pl.when(last > 0)
        def _():
            from_top.start()

        @pl.when(last == 0)
        def _():
            from_hop.start()

        for c in range(chunks):
            copy_wo(c).start()
        for i in range(span_refs):
            copy_v(i).start()
        get_probs = pltpu.make_async_copy(probs.at[micro], pb, sem_p)
        get_probs.start()
        for i in range(span_refs):
            copy_k(i).start()
        for c in range(chunks):
            copy_wq(c).start()

        from_hop.wait()
        save_up = pltpu.make_async_copy(up, u_store.at[micro], sem_out.at[0])
        save_up.start()
        def to_swap(group):
            store = s_stores[group].at[micro - live[group][0]]
            copies = [pltpu.make_async_copy(dq, store.at[0], sem_out.at[1])]
            for h in range(halves):
                start = pl.multiple_of((2 * h + other) * block, block)
                copies.append(
                    pltpu.make_async_copy(
                        up.at[:, pl.ds(start, block)], store.at[1, :, pl.ds(h * block, block)], sem_half.at[h]
                    )
                )
            return copies

        def swap_copies(do):
            for group, (first, end) in enumerate(live):

                @pl.when((micro >= first) & (micro < end))
                def _():
                    do(to_swap(group))

        swap_copies(lambda copies: [copy.start() for copy in copies[1:]])

        def project(c, carry):
            copy_wo(c).wait()
            datt[:, pl.ds(pl.multiple_of(c * wide, wide), wide)] = nn(up[...], wo[c]).astype(BF)
            return carry

        lax.fori_loop(0, chunks, project, 0)
        if head_major:
            late = [
                pltpu.make_async_copy(
                    datt.at[:, pl.ds(h * slice_w, slice_w)], d_store.at[h, micro], sem_head.at[h]
                )
                for h in range(heads)
            ]
        else:
            late = [pltpu.make_async_copy(datt, d_store.at[micro], sem_head.at[0])]
        for save in late:
            save.start()
        for i in range(span_refs):
            copy_v(i).wait()
        get_probs.wait()
        for i in range(span_refs):
            copy_k(i).wait()

        def one_group(index, carry):
            span, first = index // groups, index % groups * (pairs // groups)
            rws = pl.ds(pl.multiple_of(span * SPAN, SPAN), SPAN)
            for step in range(pairs // groups):
                pair = first + step
                cols = pl.ds(pl.multiple_of(pair * PAIR, PAIR), PAIR)
                val = jnp.concatenate([vb[span * K_NBR + k, :, cols] for k in range(K_NBR)], axis=0)
                key = jnp.concatenate([kb[span * K_NBR + k, :, cols] for k in range(K_NBR)], axis=0)
                d_probs = nt(head_rows(datt[rws, cols]), val)
                prob = pb[span * pairs + pair].astype(F32)
                delta = jnp.sum(prob * d_probs, axis=-1, keepdims=True)
                d_scores = (prob * (d_probs - delta) * SCALE).astype(BF)
                dq[rws, cols] = head_columns(nn(d_scores, key)).astype(BF)
            return carry

        lax.fori_loop(0, spans * groups, one_group, 0)

        swap_copies(lambda copies: copies[0].start())

        def back(c, carry):
            copy_wq(c).wait()
            cols = pl.ds(pl.multiple_of(c * rows, rows), rows)
            gr[:, cols] = (up[:, cols].astype(F32) + nt(dq[...], wq[c])).astype(BF)
            return carry

        lax.fori_loop(0, chunks, back, 0)
        late.append(pltpu.make_async_copy(gr, leaving, sem_out.at[2]))
        late[-1].start()
        late.append(pltpu.make_async_copy(gr, g_store.at[micro], sem_out.at[3]))
        late[-1].start()
        for save in [save_up] + late:
            save.wait()

        swap_copies(lambda copies: [copy.wait() for copy in copies])


def weight_grads_kernel(scale, par, x_own, x_got, up_own, att_own, att_got, *parts_and_out):
    parts, out_ref = parts_and_out[:-1], parts_and_out[-1]
    flat, width = att_own.shape
    output_sum = tn(up_own[...], att_own[...])
    query_sum = 0.0
    row = 0
    for dq_own, dq_got, up_got in zip(parts[::3], parts[1::3], parts[2::3]):
        count = dq_got.shape[0] * dq_got.shape[2]
        rws = slice(row, row + count)
        query_sum += tn(x_own[rws, :], dq_own[...].reshape(count, width))
        query_sum += tn(x_got[rws, :], dq_got[...].reshape(count, width))
        output_sum += tn(up_got[...].reshape(count, up_got.shape[-1]), att_got[rws, :])
        row += count
    out_ref[:, :width] = (query_sum * scale).astype(BF)
    out_ref[:, width:] = (output_sum * scale).astype(BF)


def attended_kernel(scal, values, probs, a0, a_store, vb, pb, att, sem_v, sem_p, sem_a):
    micros, tokens, width = a_store.shape
    spans = tokens // SPAN
    pairs = width // PAIR

    def get_probs(m):
        return pltpu.make_async_copy(probs.at[m], pb.at[m], sem_p.at[m])

    def put(m):
        return pltpu.make_async_copy(att.at[m], a_store.at[m], sem_a.at[m])

    @pl.when(scal[0] > 0)
    def _():
        get_values = pltpu.make_async_copy(values, vb, sem_v)
        get_values.start()
        for m in range(micros):
            get_probs(m).start()
        get_values.wait()

        def one(m, carry):
            get_probs(m).wait()
            for span in range(spans):
                rws = slice(span * SPAN, (span + 1) * SPAN)
                owners = [scal[1 + (m * spans + span) * K_NBR + k] for k in range(K_NBR)]
                for pair in range(pairs):
                    cols = slice(pair * PAIR, (pair + 1) * PAIR)
                    val = jnp.concatenate([vb[o, :, cols] for o in owners], axis=0)
                    att[m, rws, cols] = head_columns(nn(pb[m, span * pairs + pair], val)).astype(BF)
            put(m).start()
            return carry

        lax.fori_loop(0, micros, one, 0)
        for m in range(micros):
            put(m).wait()


def block_grads_kernel(micros, local, ids, mask, q_ref, d_ref, kv_ref, out_ref, acc):
    reader = pl.program_id(0)
    rows, width = d_ref.shape[1], d_ref.shape[2]
    tokens = rows // micros
    spans = tokens // SPAN
    readers = pl.num_programs(0)

    @pl.when(reader == 0)
    def _():
        acc[...] = jnp.zeros_like(acc)

    def block(r, which):
        start = pl.multiple_of((r % local * 2 + which) * NBR_LEN, NBR_LEN)
        return kv_ref[r // local, pl.ds(start, NBR_LEN), :]

    def unit(index, carry):
        at = [((index // spans * readers + reader) * spans + index % spans) * K_NBR + k for k in range(K_NBR)]
        rws = pl.ds(pl.multiple_of(index * SPAN, SPAN), SPAN)
        refs = [ids[i] for i in at]
        keep = [mask[i] > 0 for i in at]
        zero = jnp.zeros((NBR_LEN, width), BF)
        key = jnp.concatenate([jnp.where(m, block(r, 0), zero) for m, r in zip(keep, refs)], axis=0)
        val = jnp.concatenate([jnp.where(m, block(r, 1), zero) for m, r in zip(keep, refs)], axis=0)
        q_rows = head_rows(q_ref[0, rws, :])
        d_rows = head_rows(d_ref[0, rws, :])
        scores = nt(key, q_rows) * SCALE
        weights = jnp.exp(scores - jnp.max(scores, axis=0, keepdims=True))
        prob = weights / jnp.sum(weights, axis=0, keepdims=True)
        d_probs = nt(val, d_rows)
        delta = jnp.sum(prob * d_probs, axis=0, keepdims=True)
        d_scores = (prob * (d_probs - delta) * SCALE).astype(BF)
        d_keys = nn(d_scores, q_rows)
        d_values = nn(prob.astype(BF), d_rows)
        fzero = jnp.zeros((NBR_LEN, width), F32)
        for k in range(K_NBR):
            part = slice(k * NBR_LEN, (k + 1) * NBR_LEN)
            acc[refs[k], 0] += jnp.where(keep[k], d_keys[part], fzero)
            acc[refs[k], 1] += jnp.where(keep[k], d_values[part], fzero)
        return carry

    lax.fori_loop(0, micros * spans, unit, 0, unroll=4)

    @pl.when(reader == readers - 1)
    def _():
        out_ref[...] = acc[...].astype(BF)


def body(
    section_inputs,
    top_grads,
    query_weight,
    output_weight,
    neighbour_kv,
    nbr_ids,
    send_list,
    send_counts,
):
    n_section = lax.axis_size("section")
    section_index = lax.axis_index("section")
    n_data = lax.axis_size("dp")
    data_index = lax.axis_index("dp")
    inputs_all = section_inputs[0]
    w_query = query_weight[0]
    w_out = output_weight[0]
    owned = neighbour_kv[0]
    micros, tokens, model = inputs_all.shape
    blk_dev = owned.shape[0]
    width = w_query.shape[1]
    spans = tokens // SPAN
    slice_w = width // n_data
    params = functools.partial(pltpu.CompilerParams, vmem_limit_bytes=56 << 20)

    near = n_data // 2
    mates = data_index ^ jnp.arange(near, dtype=jnp.int32)

    def wanted(owner):
        row = lax.dynamic_index_in_dim(send_list, owner, 0, keepdims=False)
        counts = lax.dynamic_index_in_dim(send_counts, owner, 0, keepdims=False)
        return jnp.take(row, mates), jnp.take(counts, mates)

    wants = [wanted(data_index), wanted(data_index ^ near)]

    def across(which, behind):
        own = owned[:, which]
        if behind is not None:
            own, behind = lax.optimization_barrier((own, behind))
        return own, lax.ppermute(own, "dp", [(i, i ^ near) for i in range(n_data)])

    def picked(copies):
        pieces = []
        for k in range(near):
            piece = []
            for blocks, (which_block, counts) in zip(copies, wants):
                chosen = jnp.zeros((NBR_LEN, width), BF)
                for b in range(blk_dev):
                    chosen = jnp.where((which_block[k] == b) & (counts[k] > 0), blocks[b], chosen)
                piece.append(chosen)
            pieces.append(jnp.stack(piece))
        return pieces

    def fetch(pieces):
        moved = [lax.ppermute(pieces[k], "dp", [(i, i ^ k) for i in range(n_data)]) for k in range(1, near)]
        return jnp.concatenate(pieces[:1] + moved, axis=0)

    def exchange(x):
        return lax.all_to_all(x, "dp", split_axis=0, concat_axis=0, tiled=True)

    key_copies = across(0, None)
    value_copies = across(1, key_copies[1])
    key_pieces, inputs_all = lax.optimization_barrier((picked(key_copies), inputs_all))
    keys = fetch(key_pieces)
    query = nn(inputs_all.reshape(micros * tokens, model), w_query).astype(BF)
    held = lax.optimization_barrier((picked(value_copies), query, inputs_all, owned, nbr_ids))
    value_pieces, query, inputs_all, owned, nbr_ids = held
    values = fetch(value_pieces)
    query = query.reshape(micros, tokens, width)
    apart = (nbr_ids // blk_dev).astype(jnp.int32) ^ data_index
    owners = apart % near * 2 + apart // near

    probs = pl.pallas_call(
        probs_kernel,
        cost_estimate=cost(7),
        out_shape=jax.ShapeDtypeStruct((micros, spans * width // PAIR, 2 * SPAN, KEYS), BF),
        grid_spec=pltpu.PrefetchScalarGridSpec(
            num_scalar_prefetch=1,
            grid=(micros,),
            in_specs=[
                pl.BlockSpec((1, tokens, width), lambda i, o: (i, 0, 0)),
                pl.BlockSpec((n_data, NBR_LEN, width), lambda i, o: (0, 0, 0)),
            ],
            out_specs=pl.BlockSpec((1, spans * width // PAIR, 2 * SPAN, KEYS), lambda i, o: (i, 0, 0, 0)),
        ),
        compiler_params=params(),
    )(owners.reshape(-1), query, keys)

    def by_heads(x):
        return jnp.moveaxis(x.reshape(-1, n_data, slice_w), 1, 0)

    q_rows = micros * tokens
    kv_rows = blk_dev * 2 * NBR_LEN
    id_rows = micros * spans * K_NBR
    id_tile = jnp.broadcast_to(nbr_ids.reshape(1, id_rows, 1).astype(BF), (n_data, id_rows, slice_w))
    sliced = jnp.concatenate([by_heads(query), by_heads(owned), id_tile], axis=1)

    partners = [(i, i ^ 1) for i in range(n_data)]
    parity = data_index % 2
    flat = micros * tokens
    halves = n_data // 2
    half = model // 2
    block = model // n_data

    def swap(x):
        return lax.ppermute(x, "dp", partners)

    flat_in = inputs_all.reshape(flat, model)
    inputs_other = jnp.concatenate(
        [lax.dynamic_slice_in_dim(flat_in, (2 * h + 1 - parity) * block, block, axis=1) for h in range(halves)],
        axis=1,
    )

    chunks = 4
    ticks = micros + 2 * (n_section - 1)
    refs = spans * K_NBR
    micro_at = jnp.arange(ticks, dtype=jnp.int32) - 2 * (n_section - 1 - section_index)
    slot_at = jnp.clip(micro_at, 0, micros - 1)
    is_last = (section_index == n_section - 1).astype(jnp.int32)
    other = (1 - parity).astype(jnp.int32)
    table = jnp.concatenate(
        [
            slot_at[:, None],
            ((micro_at >= 0) & (micro_at < micros)).astype(jnp.int32)[:, None],
            jnp.broadcast_to(jnp.stack([is_last, other]), (ticks, 2)),
            jnp.take(owners.reshape(micros, refs), slot_at, axis=0),
        ],
        axis=1,
    ).astype(jnp.int32)
    scal = table.reshape(-1)
    head_major = slice_w % 128 == 0
    d_shape = (n_data, micros, tokens, slice_w) if head_major else (micros, tokens, width)
    swap_groups = [(micros - 1, micros), (micros - 2, micros - 1), (0, micros - 2)]
    store_shapes = (
        jax.ShapeDtypeStruct((micros, tokens, model), BF),
        jax.ShapeDtypeStruct((micros, tokens, model), BF),
        jax.ShapeDtypeStruct(d_shape, BF),
        *(jax.ShapeDtypeStruct((end - first, 2, tokens, width), BF) for first, end in swap_groups),
    )

    def tick(index, arriving, stores):
        live = [group for group in swap_groups if ticks - micros + group[1] > index]
        count = 3 + len(live)
        out = pl.pallas_call(
            functools.partial(tick_kernel, chunks, index * table.shape[1], head_major, live),
            out_shape=(jax.ShapeDtypeStruct((tokens, model), BF), *store_shapes[:count]),
            in_specs=[pl.BlockSpec(memory_space=pltpu.SMEM)] + [ANY] * (7 + count),
            out_specs=[ANY] * (1 + count),
            scratch_shapes=[
                pltpu.VMEM((tokens, model), BF),
                pltpu.VMEM((chunks, model, width // chunks), BF),
                pltpu.VMEM((chunks, model // chunks, width), BF),
                pltpu.VMEM((refs, NBR_LEN, width), BF),
                pltpu.VMEM((refs, NBR_LEN, width), BF),
                pltpu.VMEM((spans * width // PAIR, 2 * SPAN, KEYS), BF),
                pltpu.VMEM((tokens, width), BF),
                pltpu.VMEM((tokens, width), BF),
                pltpu.VMEM((tokens, model), BF),
                pltpu.SemaphoreType.DMA,
                pltpu.SemaphoreType.DMA((chunks,)),
                pltpu.SemaphoreType.DMA((chunks,)),
                pltpu.SemaphoreType.DMA((refs,)),
                pltpu.SemaphoreType.DMA((refs,)),
                pltpu.SemaphoreType.DMA,
                pltpu.SemaphoreType.DMA((4,)),
                pltpu.SemaphoreType.DMA((halves,)),
                pltpu.SemaphoreType.DMA((n_data if head_major else 1,)),
            ],
            input_output_aliases={8 + i: 1 + i for i in range(count)},
            cost_estimate=cost(11),
            compiler_params=params(),
        )(scal, arriving, top_grads, w_out, w_query, keys, values, probs, *stores[:count])
        return (*out, *stores[count:])

    def unwritten(*shapes):
        return pl.pallas_call(
            lambda *refs: None,
            out_shape=shapes,
            out_specs=[ANY] * len(shapes),
        )()

    def attend(enabled, store):
        return pl.pallas_call(
            attended_kernel,
            out_shape=jax.ShapeDtypeStruct((micros, tokens, width), BF),
            grid_spec=pltpu.PrefetchScalarGridSpec(
                num_scalar_prefetch=1,
                grid=(1,),
                in_specs=[ANY] * 3,
                out_specs=ANY,
                scratch_shapes=[
                    pltpu.VMEM((n_data, NBR_LEN, width), BF),
                    pltpu.VMEM((micros, spans * width // PAIR, 2 * SPAN, KEYS), BF),
                    pltpu.VMEM((micros, tokens, width), BF),
                    pltpu.SemaphoreType.DMA,
                    pltpu.SemaphoreType.DMA((micros,)),
                    pltpu.SemaphoreType.DMA((micros,)),
                ],
            ),
            input_output_aliases={3: 0},
            cost_estimate=cost(5),
            compiler_params=params(),
        )(jnp.concatenate([enabled[None].astype(jnp.int32), owners.reshape(-1)]), values, probs, store)

    *stores, attended = unwritten(*store_shapes, jax.ShapeDtypeStruct((micros, tokens, width), BF))
    arrived = [jnp.zeros((tokens, model), BF)] * 2
    got = []
    for index in range(ticks):
        if index == micros + 3:
            arrived[index], attended_got = lax.optimization_barrier((arrived[index], attended_got))
        leaving, *stores = tick(index, arrived[index], stores)
        if index == 0:
            sliced, inputs_other, leaving, attended = lax.optimization_barrier((sliced, inputs_other, leaving, attended))
            sliced = exchange(sliced)
            inputs_got = swap(inputs_other)
            attended = attend(1 - is_last, attended)
            stores[0], attended = lax.optimization_barrier((stores[0], attended))
        hops = []
        for s in range(1, n_section):
            if 0 <= index - 2 * (n_section - 1 - s) < micros:
                hops.append((s, s - 1))
        if index > 0:
            held = lax.optimization_barrier((leaving, arrived[index + 1]))
            if hops:
                leaving, arrived[index + 1] = held
        arrived.append(lax.ppermute(leaving, "section", hops) if hops else leaving)
        if index == micros:
            attended = attend(is_last, attended)
            stores[0], attended = lax.optimization_barrier((stores[0], attended))
            held = lax.optimization_barrier((arrived[index + 1], sliced, inputs_got))
            arrived[index + 1], sliced, inputs_got = held
            attended_got = swap(attended.reshape(flat, width))
        for group, (_, end) in enumerate(swap_groups):
            if end == index - (ticks - micros) + 1:
                at = 3 + group
                if hops:
                    stores[at], arrived[index + 1] = lax.optimization_barrier((stores[at], arrived[index + 1]))
                if got:
                    stores[at], got[-1] = lax.optimization_barrier((stores[at], got[-1]))
                got.append(swap(stores[at]))
    grads_in, upstream, d_store, *s_stores = stores

    grad_scale = (flat * n_data) ** (-0.5)
    parts = []
    part_specs = []
    for own, part in zip(s_stores[::-1], got):
        count = part.shape[0]
        parts += [own, part, part]
        part_specs += [
            pl.BlockSpec((count, 1, tokens, width), lambda j, p: (0, 0, 0, 0)),
            pl.BlockSpec((count, 1, tokens, width), lambda j, p: (0, 0, 0, 0)),
            pl.BlockSpec((count, 1, tokens, block), lambda j, p: (0, 1, 0, j)),
        ]
    terms = pl.pallas_call(
        functools.partial(weight_grads_kernel, grad_scale),
        cost_estimate=cost(9),
        out_shape=jax.ShapeDtypeStruct((half, 2 * width), BF),
        grid_spec=pltpu.PrefetchScalarGridSpec(
            num_scalar_prefetch=1,
            grid=(halves,),
            in_specs=[
                pl.BlockSpec((flat, block), lambda j, p: (0, 2 * j + p[0])),
                pl.BlockSpec((flat, block), lambda j, p: (0, j)),
                pl.BlockSpec((flat, block), lambda j, p: (0, 2 * j + p[0])),
                pl.BlockSpec((flat, width), lambda j, p: (0, 0)),
                pl.BlockSpec((flat, width), lambda j, p: (0, 0)),
                *part_specs,
            ],
            out_specs=pl.BlockSpec((block, 2 * width), lambda j, p: (j, 0)),
        ),
        compiler_params=params(),
    )(
        parity[None].astype(jnp.int32),
        inputs_all.reshape(flat, model),
        inputs_got,
        upstream.reshape(flat, model),
        attended.reshape(flat, width),
        attended_got,
        *parts,
    )
    d_heads = exchange(d_store) if head_major else exchange(by_heads(d_store))
    d_heads = d_heads.reshape(n_data, q_rows, slice_w)
    terms, d_heads = lax.optimization_barrier((terms, d_heads))
    shares = lax.psum_scatter(
        terms,
        "dp",
        scatter_dimension=0,
        tiled=True,
        axis_index_groups=[list(range(p, n_data, 2)) for p in range(2)],
    )

    ids_all = sliced[:, q_rows + kv_rows :, 0].astype(jnp.int32).reshape(n_data, micros, spans, K_NBR)
    ids_all = jnp.moveaxis(ids_all, 0, 1).reshape(micros, n_data * spans, K_NBR)
    owner_all = ids_all // blk_dev
    reader_all = (jnp.arange(n_data * spans, dtype=jnp.int32) // spans)[None, :, None]
    hit_owner = owner_all[..., None] == jnp.arange(n_data, dtype=jnp.int32)
    list_r = jnp.take(send_list, reader_all[0, :, 0], axis=1).T[None, :, None, :]
    count_r = jnp.take(send_counts, reader_all[0, :, 0], axis=1).T[None, :, None, :]
    block_all = owner_all * blk_dev + jnp.sum(jnp.where(hit_owner, list_r, 0), axis=-1)
    mask_all = jnp.sum(jnp.where(hit_owner, count_r, 0), axis=-1)
    blocks = n_data * blk_dev
    block_grads = pl.pallas_call(
        functools.partial(block_grads_kernel, micros, blk_dev),
        cost_estimate=cost(37),
        out_shape=jax.ShapeDtypeStruct((blocks, 2, NBR_LEN, slice_w), BF),
        grid_spec=pltpu.PrefetchScalarGridSpec(
            num_scalar_prefetch=2,
            grid=(n_data,),
            in_specs=[
                pl.BlockSpec((1, q_rows, slice_w), lambda i, a, b: (i, 0, 0)),
                pl.BlockSpec((1, q_rows, slice_w), lambda i, a, b: (i, 0, 0)),
                pl.BlockSpec((n_data, kv_rows, slice_w), lambda i, a, b: (0, q_rows // kv_rows, 0)),
            ],
            out_specs=pl.BlockSpec((blocks, 2, NBR_LEN, slice_w), lambda i, a, b: (0, 0, 0, 0)),
            scratch_shapes=[pltpu.VMEM((blocks, 2, NBR_LEN, slice_w), F32)],
        ),
        compiler_params=params(),
    )(block_all.reshape(-1).astype(jnp.int32), mask_all.reshape(-1).astype(jnp.int32), sliced, d_heads, sliced)
    returned = exchange(block_grads.reshape(n_data, blk_dev, 2, NBR_LEN, slice_w))
    kv_grads = jnp.moveaxis(returned, 0, -2).reshape(blk_dev, 2, NBR_LEN, width)
    return (
        grads_in[None],
        shares[None, :, :width],
        shares[None, :, width:],
        kv_grads[None],
    )


def solution(mesh):
    in_specs = (
        P("section", None, "dp", None),
        P(None, "dp", None),
        P("section", None, None),
        P("section", None, None),
        P("section", "dp", None, None, None),
        P(None, "dp", None),
        P(),
        P(),
    )
    out_specs = (
        P("section", None, "dp", None),
        P("section", "dp", None),
        P("section", "dp", None),
        P("section", "dp", None, None, None),
    )
    return jax.shard_map(body, mesh=mesh, in_specs=in_specs, out_specs=out_specs, check_vma=False)
```

```python
import functools

import jax
import jax.numpy as jnp
from jax import lax
from jax.experimental import pallas as pl
from jax.experimental.pallas import tpu as pltpu
from jax.sharding import PartitionSpec as P

HEADS = 16
HEAD_DIM = 64
SPAN = 64
K_NBR = 2
NBR_LEN = 128
PAIR = 2 * HEAD_DIM
KEYS = K_NBR * NBR_LEN
SCALE = HEAD_DIM ** (-0.5)
BF = jnp.bfloat16
F32 = jnp.float32
ANY = pl.BlockSpec(memory_space=pl.ANY)


def cost(micros_of_work):
    return pl.CostEstimate(flops=0, transcendentals=0, bytes_accessed=int(micros_of_work * 3.6e6))


def nt(a, b):
    return lax.dot_general(a, b, (((1,), (1,)), ((), ())), preferred_element_type=F32)


def nn(a, b):
    return lax.dot_general(a, b, (((1,), (0,)), ((), ())), preferred_element_type=F32)


def tn(a, b):
    return lax.dot_general(a, b, (((0,), (0,)), ((), ())), preferred_element_type=F32)


def head_rows(x):
    heads = x.shape[1] // HEAD_DIM
    if heads == 1:
        return x
    lane = lax.broadcasted_iota(jnp.int32, x.shape, 1) // HEAD_DIM
    zero = jnp.zeros_like(x)
    return jnp.concatenate([jnp.where(lane == h, x, zero) for h in range(heads)], axis=0)


def head_columns(y):
    heads = y.shape[1] // HEAD_DIM
    out = y[:SPAN]
    lane = lax.broadcasted_iota(jnp.int32, out.shape, 1) // HEAD_DIM
    for h in range(1, heads):
        out = jnp.where(lane == h, y[h * SPAN : (h + 1) * SPAN], out)
    return out


def softmax_rows(scores):
    weights = jnp.exp(scores - jnp.max(scores, axis=-1, keepdims=True))
    return weights / jnp.sum(weights, axis=-1, keepdims=True)


def probs_kernel(owners, q_ref, k_ref, out_ref):
    micro = pl.program_id(0)
    tokens, width = q_ref.shape[1], q_ref.shape[2]
    spans = tokens // SPAN
    for span in range(spans):
        refs = [owners[(micro * spans + span) * K_NBR + k] for k in range(K_NBR)]
        for pair in range(width // PAIR):
            cols = slice(pair * PAIR, (pair + 1) * PAIR)
            keys = jnp.concatenate([k_ref[r, :, cols] for r in refs], axis=0)
            rows = head_rows(q_ref[0, span * SPAN : (span + 1) * SPAN, cols])
            out_ref[0, span * (width // PAIR) + pair] = softmax_rows(nt(rows, keys) * SCALE).astype(BF)


def tick_kernel(
    chunks, base, head_major, live,
    scal,
    arriving, top, w_out, w_query, keys, values, probs,
    *refs,
):
    count = 3 + len(live)
    leaving, g_store, u_store, d_store, *s_stores = refs[count : 2 * count + 1]
    (
        up, wo, wq, kb, vb, pb, datt, dq, gr,
        sem_up, sem_wo, sem_wq, sem_k, sem_v, sem_p, sem_out, sem_half, sem_head,
    ) = refs[2 * count + 1 :]
    micro = scal[base]
    valid = scal[base + 1]
    last = scal[base + 2]
    other = scal[base + 3]
    tokens, model = up.shape
    width = datt.shape[1]
    spans = tokens // SPAN
    span_refs = spans * K_NBR
    pairs = width // PAIR
    rows = model // chunks
    wide = width // chunks
    groups = 1
    halves = sem_half.shape[0]
    block = model // (2 * halves)
    heads = sem_head.shape[0]
    slice_w = width // heads

    def copy_wo(c):
        return pltpu.make_async_copy(w_out.at[:, pl.ds(c * wide, wide)], wo.at[c], sem_wo.at[c])

    def copy_wq(c):
        return pltpu.make_async_copy(w_query.at[pl.ds(c * rows, rows)], wq.at[c], sem_wq.at[c])

    def copy_v(i):
        return pltpu.make_async_copy(values.at[scal[base + 4 + i]], vb.at[i], sem_v.at[i])

    def copy_k(i):
        return pltpu.make_async_copy(keys.at[scal[base + 4 + i]], kb.at[i], sem_k.at[i])

    @pl.when(valid > 0)
    def _():
        from_top = pltpu.make_async_copy(top.at[micro], up, sem_up)
        from_hop = pltpu.make_async_copy(arriving, up, sem_up)

        @pl.when(last > 0)
        def _():
            from_top.start()

        @pl.when(last == 0)
        def _():
            from_hop.start()

        for c in range(chunks):
            copy_wo(c).start()
        for i in range(span_refs):
            copy_v(i).start()
        get_probs = pltpu.make_async_copy(probs.at[micro], pb, sem_p)
        get_probs.start()
        for i in range(span_refs):
            copy_k(i).start()
        for c in range(chunks):
            copy_wq(c).start()

        from_hop.wait()
        save_up = pltpu.make_async_copy(up, u_store.at[micro], sem_out.at[0])
        save_up.start()
        def to_swap(group):
            store = s_stores[group].at[micro - live[group][0]]
            copies = [pltpu.make_async_copy(dq, store.at[0], sem_out.at[1])]
            for h in range(halves):
                start = pl.multiple_of((2 * h + other) * block, block)
                copies.append(
                    pltpu.make_async_copy(
                        up.at[:, pl.ds(start, block)], store.at[1, :, pl.ds(h * block, block)], sem_half.at[h]
                    )
                )
            return copies

        def swap_copies(do):
            for group, (first, end) in enumerate(live):

                @pl.when((micro >= first) & (micro < end))
                def _():
                    do(to_swap(group))

        swap_copies(lambda copies: [copy.start() for copy in copies[1:]])

        def project(c, carry):
            copy_wo(c).wait()
            datt[:, pl.ds(pl.multiple_of(c * wide, wide), wide)] = nn(up[...], wo[c]).astype(BF)
            return carry

        lax.fori_loop(0, chunks, project, 0)
        if head_major:
            late = [
                pltpu.make_async_copy(
                    datt.at[:, pl.ds(h * slice_w, slice_w)], d_store.at[h, micro], sem_head.at[h]
                )
                for h in range(heads)
            ]
        else:
            late = [pltpu.make_async_copy(datt, d_store.at[micro], sem_head.at[0])]
        for save in late:
            save.start()
        for i in range(span_refs):
            copy_v(i).wait()
        get_probs.wait()
        for i in range(span_refs):
            copy_k(i).wait()

        def one_group(index, carry):
            span, first = index // groups, index % groups * (pairs // groups)
            rws = pl.ds(pl.multiple_of(span * SPAN, SPAN), SPAN)
            for step in range(pairs // groups):
                pair = first + step
                cols = pl.ds(pl.multiple_of(pair * PAIR, PAIR), PAIR)
                val = jnp.concatenate([vb[span * K_NBR + k, :, cols] for k in range(K_NBR)], axis=0)
                key = jnp.concatenate([kb[span * K_NBR + k, :, cols] for k in range(K_NBR)], axis=0)
                d_probs = nt(head_rows(datt[rws, cols]), val)
                prob = pb[span * pairs + pair].astype(F32)
                delta = jnp.sum(prob * d_probs, axis=-1, keepdims=True)
                d_scores = (prob * (d_probs - delta) * SCALE).astype(BF)
                dq[rws, cols] = head_columns(nn(d_scores, key)).astype(BF)
            return carry

        lax.fori_loop(0, spans * groups, one_group, 0)

        swap_copies(lambda copies: copies[0].start())

        def back(c, carry):
            copy_wq(c).wait()
            cols = pl.ds(pl.multiple_of(c * rows, rows), rows)
            gr[:, cols] = (up[:, cols].astype(F32) + nt(dq[...], wq[c])).astype(BF)
            return carry

        lax.fori_loop(0, chunks, back, 0)
        late.append(pltpu.make_async_copy(gr, leaving, sem_out.at[2]))
        late[-1].start()
        late.append(pltpu.make_async_copy(gr, g_store.at[micro], sem_out.at[3]))
        late[-1].start()
        for save in [save_up] + late:
            save.wait()

        swap_copies(lambda copies: [copy.wait() for copy in copies])


def weight_grads_kernel(scale, par, x_own, x_got, up_own, att_own, att_got, *parts_and_out):
    parts, out_ref = parts_and_out[:-1], parts_and_out[-1]
    flat, width = att_own.shape
    output_sum = tn(up_own[...], att_own[...])
    query_sum = 0.0
    row = 0
    for dq_own, dq_got, up_got in zip(parts[::3], parts[1::3], parts[2::3]):
        count = dq_got.shape[0] * dq_got.shape[2]
        rws = slice(row, row + count)
        query_sum += tn(x_own[rws, :], dq_own[...].reshape(count, width))
        query_sum += tn(x_got[rws, :], dq_got[...].reshape(count, width))
        output_sum += tn(up_got[...].reshape(count, up_got.shape[-1]), att_got[rws, :])
        row += count
    out_ref[:, :width] = (query_sum * scale).astype(BF)
    out_ref[:, width:] = (output_sum * scale).astype(BF)


def attended_kernel(scal, values, probs, a0, a_store, vb, pb, att, sem_v, sem_p, sem_a):
    micros, tokens, width = a_store.shape
    spans = tokens // SPAN
    pairs = width // PAIR

    def get_probs(m):
        return pltpu.make_async_copy(probs.at[m], pb.at[m], sem_p.at[m])

    def put(m):
        return pltpu.make_async_copy(att.at[m], a_store.at[m], sem_a.at[m])

    @pl.when(scal[0] > 0)
    def _():
        get_values = pltpu.make_async_copy(values, vb, sem_v)
        get_values.start()
        for m in range(micros):
            get_probs(m).start()
        get_values.wait()

        def one(m, carry):
            get_probs(m).wait()
            for span in range(spans):
                rws = slice(span * SPAN, (span + 1) * SPAN)
                owners = [scal[1 + (m * spans + span) * K_NBR + k] for k in range(K_NBR)]
                for pair in range(pairs):
                    cols = slice(pair * PAIR, (pair + 1) * PAIR)
                    val = jnp.concatenate([vb[o, :, cols] for o in owners], axis=0)
                    att[m, rws, cols] = head_columns(nn(pb[m, span * pairs + pair], val)).astype(BF)
            put(m).start()
            return carry

        lax.fori_loop(0, micros, one, 0)
        for m in range(micros):
            put(m).wait()


def block_grads_kernel(micros, local, ids, mask, q_ref, d_ref, kv_ref, out_ref, acc):
    reader = pl.program_id(0)
    rows, width = d_ref.shape[1], d_ref.shape[2]
    tokens = rows // micros
    spans = tokens // SPAN
    readers = pl.num_programs(0)

    @pl.when(reader == 0)
    def _():
        acc[...] = jnp.zeros_like(acc)

    def block(r, which):
        start = pl.multiple_of((r % local * 2 + which) * NBR_LEN, NBR_LEN)
        return kv_ref[r // local, pl.ds(start, NBR_LEN), :]

    def unit(index, carry):
        at = [((index // spans * readers + reader) * spans + index % spans) * K_NBR + k for k in range(K_NBR)]
        rws = pl.ds(pl.multiple_of(index * SPAN, SPAN), SPAN)
        refs = [ids[i] for i in at]
        keep = [mask[i] > 0 for i in at]
        zero = jnp.zeros((NBR_LEN, width), BF)
        key = jnp.concatenate([jnp.where(m, block(r, 0), zero) for m, r in zip(keep, refs)], axis=0)
        val = jnp.concatenate([jnp.where(m, block(r, 1), zero) for m, r in zip(keep, refs)], axis=0)
        q_rows = head_rows(q_ref[0, rws, :])
        d_rows = head_rows(d_ref[0, rws, :])
        scores = nt(key, q_rows) * SCALE
        weights = jnp.exp(scores - jnp.max(scores, axis=0, keepdims=True))
        prob = weights / jnp.sum(weights, axis=0, keepdims=True)
        d_probs = nt(val, d_rows)
        delta = jnp.sum(prob * d_probs, axis=0, keepdims=True)
        d_scores = (prob * (d_probs - delta) * SCALE).astype(BF)
        d_keys = nn(d_scores, q_rows)
        d_values = nn(prob.astype(BF), d_rows)
        fzero = jnp.zeros((NBR_LEN, width), F32)
        for k in range(K_NBR):
            part = slice(k * NBR_LEN, (k + 1) * NBR_LEN)
            acc[refs[k], 0] += jnp.where(keep[k], d_keys[part], fzero)
            acc[refs[k], 1] += jnp.where(keep[k], d_values[part], fzero)
        return carry

    lax.fori_loop(0, micros * spans, unit, 0, unroll=4)

    @pl.when(reader == readers - 1)
    def _():
        out_ref[...] = acc[...].astype(BF)


def body(
    section_inputs,
    top_grads,
    query_weight,
    output_weight,
    neighbour_kv,
    nbr_ids,
    send_list,
    send_counts,
):
    n_section = lax.axis_size("section")
    section_index = lax.axis_index("section")
    n_data = lax.axis_size("dp")
    data_index = lax.axis_index("dp")
    inputs_all = section_inputs[0]
    w_query = query_weight[0]
    w_out = output_weight[0]
    owned = neighbour_kv[0]
    micros, tokens, model = inputs_all.shape
    blk_dev = owned.shape[0]
    width = w_query.shape[1]
    spans = tokens // SPAN
    slice_w = width // n_data
    params = functools.partial(pltpu.CompilerParams, vmem_limit_bytes=56 << 20)

    near = n_data // 2
    mates = data_index ^ jnp.arange(near, dtype=jnp.int32)

    def wanted(owner):
        row = lax.dynamic_index_in_dim(send_list, owner, 0, keepdims=False)
        counts = lax.dynamic_index_in_dim(send_counts, owner, 0, keepdims=False)
        return jnp.take(row, mates), jnp.take(counts, mates)

    wants = [wanted(data_index), wanted(data_index ^ near)]

    def across(which, behind):
        own = owned[:, which]
        if behind is not None:
            own, behind = lax.optimization_barrier((own, behind))
        return own, lax.ppermute(own, "dp", [(i, i ^ near) for i in range(n_data)])

    def picked(copies):
        pieces = []
        for k in range(near):
            piece = []
            for blocks, (which_block, counts) in zip(copies, wants):
                chosen = jnp.zeros((NBR_LEN, width), BF)
                for b in range(blk_dev):
                    chosen = jnp.where((which_block[k] == b) & (counts[k] > 0), blocks[b], chosen)
                piece.append(chosen)
            pieces.append(jnp.stack(piece))
        return pieces

    def fetch(pieces):
        moved = [lax.ppermute(pieces[k], "dp", [(i, i ^ k) for i in range(n_data)]) for k in range(1, near)]
        return jnp.concatenate(pieces[:1] + moved, axis=0)

    def exchange(x):
        return lax.all_to_all(x, "dp", split_axis=0, concat_axis=0, tiled=True)

    key_copies = across(0, None)
    value_copies = across(1, key_copies[1])
    key_pieces, inputs_all = lax.optimization_barrier((picked(key_copies), inputs_all))
    keys = fetch(key_pieces)
    query = nn(inputs_all.reshape(micros * tokens, model), w_query).astype(BF)
    held = lax.optimization_barrier((picked(value_copies), query, inputs_all, owned, nbr_ids))
    value_pieces, query, inputs_all, owned, nbr_ids = held
    values = fetch(value_pieces)
    query = query.reshape(micros, tokens, width)
    apart = (nbr_ids // blk_dev).astype(jnp.int32) ^ data_index
    owners = apart % near * 2 + apart // near

    probs = pl.pallas_call(
        probs_kernel,
        cost_estimate=cost(7),
        out_shape=jax.ShapeDtypeStruct((micros, spans * width // PAIR, 2 * SPAN, KEYS), BF),
        grid_spec=pltpu.PrefetchScalarGridSpec(
            num_scalar_prefetch=1,
            grid=(micros,),
            in_specs=[
                pl.BlockSpec((1, tokens, width), lambda i, o: (i, 0, 0)),
                pl.BlockSpec((n_data, NBR_LEN, width), lambda i, o: (0, 0, 0)),
            ],
            out_specs=pl.BlockSpec((1, spans * width // PAIR, 2 * SPAN, KEYS), lambda i, o: (i, 0, 0, 0)),
        ),
        compiler_params=params(),
    )(owners.reshape(-1), query, keys)

    def by_heads(x):
        return jnp.moveaxis(x.reshape(-1, n_data, slice_w), 1, 0)

    q_rows = micros * tokens
    kv_rows = blk_dev * 2 * NBR_LEN
    id_rows = micros * spans * K_NBR
    id_tile = jnp.broadcast_to(nbr_ids.reshape(1, id_rows, 1).astype(BF), (n_data, id_rows, slice_w))
    sliced = jnp.concatenate([by_heads(query), by_heads(owned), id_tile], axis=1)

    partners = [(i, i ^ 1) for i in range(n_data)]
    parity = data_index % 2
    flat = micros * tokens
    halves = n_data // 2
    half = model // 2
    block = model // n_data

    def swap(x):
        return lax.ppermute(x, "dp", partners)

    flat_in = inputs_all.reshape(flat, model)
    inputs_other = jnp.concatenate(
        [lax.dynamic_slice_in_dim(flat_in, (2 * h + 1 - parity) * block, block, axis=1) for h in range(halves)],
        axis=1,
    )

    chunks = 4
    ticks = micros + 2 * (n_section - 1)
    refs = spans * K_NBR
    micro_at = jnp.arange(ticks, dtype=jnp.int32) - 2 * (n_section - 1 - section_index)
    slot_at = jnp.clip(micro_at, 0, micros - 1)
    is_last = (section_index == n_section - 1).astype(jnp.int32)
    other = (1 - parity).astype(jnp.int32)
    table = jnp.concatenate(
        [
            slot_at[:, None],
            ((micro_at >= 0) & (micro_at < micros)).astype(jnp.int32)[:, None],
            jnp.broadcast_to(jnp.stack([is_last, other]), (ticks, 2)),
            jnp.take(owners.reshape(micros, refs), slot_at, axis=0),
        ],
        axis=1,
    ).astype(jnp.int32)
    scal = table.reshape(-1)
    head_major = slice_w % 128 == 0
    d_shape = (n_data, micros, tokens, slice_w) if head_major else (micros, tokens, width)
    swap_groups = [(micros - 1, micros), (micros - 2, micros - 1), (0, micros - 2)]
    store_shapes = (
        jax.ShapeDtypeStruct((micros, tokens, model), BF),
        jax.ShapeDtypeStruct((micros, tokens, model), BF),
        jax.ShapeDtypeStruct(d_shape, BF),
        *(jax.ShapeDtypeStruct((end - first, 2, tokens, width), BF) for first, end in swap_groups),
    )

    def tick(index, arriving, stores):
        live = [group for group in swap_groups if ticks - micros + group[1] > index]
        count = 3 + len(live)
        out = pl.pallas_call(
            functools.partial(tick_kernel, chunks, index * table.shape[1], head_major, live),
            out_shape=(jax.ShapeDtypeStruct((tokens, model), BF), *store_shapes[:count]),
            in_specs=[pl.BlockSpec(memory_space=pltpu.SMEM)] + [ANY] * (7 + count),
            out_specs=[ANY] * (1 + count),
            scratch_shapes=[
                pltpu.VMEM((tokens, model), BF),
                pltpu.VMEM((chunks, model, width // chunks), BF),
                pltpu.VMEM((chunks, model // chunks, width), BF),
                pltpu.VMEM((refs, NBR_LEN, width), BF),
                pltpu.VMEM((refs, NBR_LEN, width), BF),
                pltpu.VMEM((spans * width // PAIR, 2 * SPAN, KEYS), BF),
                pltpu.VMEM((tokens, width), BF),
                pltpu.VMEM((tokens, width), BF),
                pltpu.VMEM((tokens, model), BF),
                pltpu.SemaphoreType.DMA,
                pltpu.SemaphoreType.DMA((chunks,)),
                pltpu.SemaphoreType.DMA((chunks,)),
                pltpu.SemaphoreType.DMA((refs,)),
                pltpu.SemaphoreType.DMA((refs,)),
                pltpu.SemaphoreType.DMA,
                pltpu.SemaphoreType.DMA((4,)),
                pltpu.SemaphoreType.DMA((halves,)),
                pltpu.SemaphoreType.DMA((n_data if head_major else 1,)),
            ],
            input_output_aliases={8 + i: 1 + i for i in range(count)},
            cost_estimate=cost(11),
            compiler_params=params(),
        )(scal, arriving, top_grads, w_out, w_query, keys, values, probs, *stores[:count])
        return (*out, *stores[count:])

    def unwritten(*shapes):
        return pl.pallas_call(
            lambda *refs: None,
            out_shape=shapes,
            out_specs=[ANY] * len(shapes),
        )()

    def attend(enabled, store):
        return pl.pallas_call(
            attended_kernel,
            out_shape=jax.ShapeDtypeStruct((micros, tokens, width), BF),
            grid_spec=pltpu.PrefetchScalarGridSpec(
                num_scalar_prefetch=1,
                grid=(1,),
                in_specs=[ANY] * 3,
                out_specs=ANY,
                scratch_shapes=[
                    pltpu.VMEM((n_data, NBR_LEN, width), BF),
                    pltpu.VMEM((micros, spans * width // PAIR, 2 * SPAN, KEYS), BF),
                    pltpu.VMEM((micros, tokens, width), BF),
                    pltpu.SemaphoreType.DMA,
                    pltpu.SemaphoreType.DMA((micros,)),
                    pltpu.SemaphoreType.DMA((micros,)),
                ],
            ),
            input_output_aliases={3: 0},
            cost_estimate=cost(5),
            compiler_params=params(),
        )(jnp.concatenate([enabled[None].astype(jnp.int32), owners.reshape(-1)]), values, probs, store)

    *stores, attended = unwritten(*store_shapes, jax.ShapeDtypeStruct((micros, tokens, width), BF))
    arrived = [jnp.zeros((tokens, model), BF)] * 2
    got = []
    for index in range(ticks):
        if index == micros + 3:
            arrived[index], attended_got = lax.optimization_barrier((arrived[index], attended_got))
        leaving, *stores = tick(index, arrived[index], stores)
        if index == 0:
            sliced, inputs_other, leaving, attended = lax.optimization_barrier((sliced, inputs_other, leaving, attended))
            sliced = exchange(sliced)
            inputs_got = swap(inputs_other)
            attended = attend(1 - is_last, attended)
            stores[0], attended = lax.optimization_barrier((stores[0], attended))
        hops = []
        for s in range(1, n_section):
            if 0 <= index - 2 * (n_section - 1 - s) < micros:
                hops.append((s, s - 1))
        if index > 0:
            held = lax.optimization_barrier((leaving, arrived[index + 1]))
            if hops:
                leaving, arrived[index + 1] = held
        arrived.append(lax.ppermute(leaving, "section", hops) if hops else leaving)
        if index == micros:
            attended = attend(is_last, attended)
            stores[0], attended = lax.optimization_barrier((stores[0], attended))
            held = lax.optimization_barrier((arrived[index + 1], sliced, inputs_got))
            arrived[index + 1], sliced, inputs_got = held
            attended_got = swap(attended.reshape(flat, width))
        for group, (_, end) in enumerate(swap_groups):
            if end == index - (ticks - micros) + 1:
                at = 3 + group
                if hops:
                    stores[at], arrived[index + 1] = lax.optimization_barrier((stores[at], arrived[index + 1]))
                if group == 0:
                    stores[at], got = lax.optimization_barrier((stores[at], got))
                got.append(swap(stores[at]))
    grads_in, upstream, d_store, *s_stores = stores
    got[-1], d_store = lax.optimization_barrier((got[-1], d_store))

    grad_scale = (flat * n_data) ** (-0.5)
    parts = []
    part_specs = []
    for own, part in zip(s_stores[::-1], got):
        count = part.shape[0]
        parts += [own, part, part]
        part_specs += [
            pl.BlockSpec((count, 1, tokens, width), lambda j, p: (0, 0, 0, 0)),
            pl.BlockSpec((count, 1, tokens, width), lambda j, p: (0, 0, 0, 0)),
            pl.BlockSpec((count, 1, tokens, block), lambda j, p: (0, 1, 0, j)),
        ]
    terms = pl.pallas_call(
        functools.partial(weight_grads_kernel, grad_scale),
        cost_estimate=cost(9),
        out_shape=jax.ShapeDtypeStruct((half, 2 * width), BF),
        grid_spec=pltpu.PrefetchScalarGridSpec(
            num_scalar_prefetch=1,
            grid=(halves,),
            in_specs=[
                pl.BlockSpec((flat, block), lambda j, p: (0, 2 * j + p[0])),
                pl.BlockSpec((flat, block), lambda j, p: (0, j)),
                pl.BlockSpec((flat, block), lambda j, p: (0, 2 * j + p[0])),
                pl.BlockSpec((flat, width), lambda j, p: (0, 0)),
                pl.BlockSpec((flat, width), lambda j, p: (0, 0)),
                *part_specs,
            ],
            out_specs=pl.BlockSpec((block, 2 * width), lambda j, p: (j, 0)),
        ),
        compiler_params=params(),
    )(
        parity[None].astype(jnp.int32),
        inputs_all.reshape(flat, model),
        inputs_got,
        upstream.reshape(flat, model),
        attended.reshape(flat, width),
        attended_got,
        *parts,
    )
    d_heads = exchange(d_store) if head_major else exchange(by_heads(d_store))
    d_heads = d_heads.reshape(n_data, q_rows, slice_w)
    terms, d_heads = lax.optimization_barrier((terms, d_heads))
    shares = lax.psum_scatter(
        terms,
        "dp",
        scatter_dimension=0,
        tiled=True,
        axis_index_groups=[list(range(p, n_data, 2)) for p in range(2)],
    )

    ids_all = sliced[:, q_rows + kv_rows :, 0].astype(jnp.int32).reshape(n_data, micros, spans, K_NBR)
    ids_all = jnp.moveaxis(ids_all, 0, 1).reshape(micros, n_data * spans, K_NBR)
    owner_all = ids_all // blk_dev
    reader_all = (jnp.arange(n_data * spans, dtype=jnp.int32) // spans)[None, :, None]
    hit_owner = owner_all[..., None] == jnp.arange(n_data, dtype=jnp.int32)
    list_r = jnp.take(send_list, reader_all[0, :, 0], axis=1).T[None, :, None, :]
    count_r = jnp.take(send_counts, reader_all[0, :, 0], axis=1).T[None, :, None, :]
    block_all = owner_all * blk_dev + jnp.sum(jnp.where(hit_owner, list_r, 0), axis=-1)
    mask_all = jnp.sum(jnp.where(hit_owner, count_r, 0), axis=-1)
    blocks = n_data * blk_dev
    block_grads = pl.pallas_call(
        functools.partial(block_grads_kernel, micros, blk_dev),
        cost_estimate=cost(37),
        out_shape=jax.ShapeDtypeStruct((blocks, 2, NBR_LEN, slice_w), BF),
        grid_spec=pltpu.PrefetchScalarGridSpec(
            num_scalar_prefetch=2,
            grid=(n_data,),
            in_specs=[
                pl.BlockSpec((1, q_rows, slice_w), lambda i, a, b: (i, 0, 0)),
                pl.BlockSpec((1, q_rows, slice_w), lambda i, a, b: (i, 0, 0)),
                pl.BlockSpec((n_data, kv_rows, slice_w), lambda i, a, b: (0, q_rows // kv_rows, 0)),
            ],
            out_specs=pl.BlockSpec((blocks, 2, NBR_LEN, slice_w), lambda i, a, b: (0, 0, 0, 0)),
            scratch_shapes=[pltpu.VMEM((blocks, 2, NBR_LEN, slice_w), F32)],
        ),
        compiler_params=params(),
    )(block_all.reshape(-1).astype(jnp.int32), mask_all.reshape(-1).astype(jnp.int32), sliced, d_heads, sliced)
    returned = exchange(block_grads.reshape(n_data, blk_dev, 2, NBR_LEN, slice_w))
    kv_grads = jnp.moveaxis(returned, 0, -2).reshape(blk_dev, 2, NBR_LEN, width)
    return (
        grads_in[None],
        shares[None, :, :width],
        shares[None, :, width:],
        kv_grads[None],
    )


def solution(mesh):
    in_specs = (
        P("section", None, "dp", None),
        P(None, "dp", None),
        P("section", None, None),
        P("section", None, None),
        P("section", "dp", None, None, None),
        P(None, "dp", None),
        P(),
        P(),
    )
    out_specs = (
        P("section", None, "dp", None),
        P("section", "dp", None),
        P("section", "dp", None),
        P("section", "dp", None, None, None),
    )
    return jax.shard_map(body, mesh=mesh, in_specs=in_specs, out_specs=out_specs, check_vma=False)
```

```python
import functools

import jax
import jax.numpy as jnp
from jax import lax
from jax.experimental import pallas as pl
from jax.experimental.pallas import tpu as pltpu
from jax.sharding import PartitionSpec as P

HEADS = 16
HEAD_DIM = 64
SPAN = 64
K_NBR = 2
NBR_LEN = 128
PAIR = 2 * HEAD_DIM
KEYS = K_NBR * NBR_LEN
SCALE = HEAD_DIM ** (-0.5)
BF = jnp.bfloat16
F32 = jnp.float32
ANY = pl.BlockSpec(memory_space=pl.ANY)


def cost(micros_of_work):
    return pl.CostEstimate(flops=0, transcendentals=0, bytes_accessed=int(micros_of_work * 3.6e6))


def nt(a, b):
    return lax.dot_general(a, b, (((1,), (1,)), ((), ())), preferred_element_type=F32)


def nn(a, b):
    return lax.dot_general(a, b, (((1,), (0,)), ((), ())), preferred_element_type=F32)


def tn(a, b):
    return lax.dot_general(a, b, (((0,), (0,)), ((), ())), preferred_element_type=F32)


def head_rows(x):
    heads = x.shape[1] // HEAD_DIM
    if heads == 1:
        return x
    lane = lax.broadcasted_iota(jnp.int32, x.shape, 1) // HEAD_DIM
    zero = jnp.zeros_like(x)
    return jnp.concatenate([jnp.where(lane == h, x, zero) for h in range(heads)], axis=0)


def head_columns(y):
    heads = y.shape[1] // HEAD_DIM
    out = y[:SPAN]
    lane = lax.broadcasted_iota(jnp.int32, out.shape, 1) // HEAD_DIM
    for h in range(1, heads):
        out = jnp.where(lane == h, y[h * SPAN : (h + 1) * SPAN], out)
    return out


def softmax_rows(scores):
    weights = jnp.exp(scores - jnp.max(scores, axis=-1, keepdims=True))
    return weights / jnp.sum(weights, axis=-1, keepdims=True)


def probs_kernel(owners, q_ref, k_ref, out_ref):
    micro = pl.program_id(0)
    tokens, width = q_ref.shape[1], q_ref.shape[2]
    spans = tokens // SPAN
    for span in range(spans):
        refs = [owners[(micro * spans + span) * K_NBR + k] for k in range(K_NBR)]
        for pair in range(width // PAIR):
            cols = slice(pair * PAIR, (pair + 1) * PAIR)
            keys = jnp.concatenate([k_ref[r, :, cols] for r in refs], axis=0)
            rows = head_rows(q_ref[0, span * SPAN : (span + 1) * SPAN, cols])
            out_ref[0, span * (width // PAIR) + pair] = softmax_rows(nt(rows, keys) * SCALE).astype(BF)


def tick_kernel(
    chunks, base, head_major, live,
    scal,
    arriving, top, w_out, w_query, keys, values, probs,
    *refs,
):
    count = 3 + len(live)
    leaving, g_store, u_store, d_store, *s_stores = refs[count : 2 * count + 1]
    (
        up, wo, wq, kb, vb, pb, datt, dq, gr,
        sem_up, sem_wo, sem_wq, sem_k, sem_v, sem_p, sem_out, sem_half, sem_head,
    ) = refs[2 * count + 1 :]
    micro = scal[base]
    valid = scal[base + 1]
    last = scal[base + 2]
    other = scal[base + 3]
    tokens, model = up.shape
    width = datt.shape[1]
    spans = tokens // SPAN
    span_refs = spans * K_NBR
    pairs = width // PAIR
    rows = model // chunks
    wide = width // chunks
    groups = 1
    halves = sem_half.shape[0]
    block = model // (2 * halves)
    heads = sem_head.shape[0]
    slice_w = width // heads

    def copy_wo(c):
        return pltpu.make_async_copy(w_out.at[:, pl.ds(c * wide, wide)], wo.at[c], sem_wo.at[c])

    def copy_wq(c):
        return pltpu.make_async_copy(w_query.at[pl.ds(c * rows, rows)], wq.at[c], sem_wq.at[c])

    def copy_v(i):
        return pltpu.make_async_copy(values.at[scal[base + 4 + i]], vb.at[i], sem_v.at[i])

    def copy_k(i):
        return pltpu.make_async_copy(keys.at[scal[base + 4 + i]], kb.at[i], sem_k.at[i])

    @pl.when(valid > 0)
    def _():
        from_top = pltpu.make_async_copy(top.at[micro], up, sem_up)
        from_hop = pltpu.make_async_copy(arriving, up, sem_up)

        @pl.when(last > 0)
        def _():
            from_top.start()

        @pl.when(last == 0)
        def _():
            from_hop.start()

        for c in range(chunks):
            copy_wo(c).start()
        for i in range(span_refs):
            copy_v(i).start()
        get_probs = pltpu.make_async_copy(probs.at[micro], pb, sem_p)
        get_probs.start()
        for i in range(span_refs):
            copy_k(i).start()
        for c in range(chunks):
            copy_wq(c).start()

        from_hop.wait()
        save_up = pltpu.make_async_copy(up, u_store.at[micro], sem_out.at[0])
        save_up.start()
        def to_swap(group):
            store = s_stores[group].at[micro - live[group][0]]
            copies = [pltpu.make_async_copy(dq, store.at[0], sem_out.at[1])]
            for h in range(halves):
                start = pl.multiple_of((2 * h + other) * block, block)
                copies.append(
                    pltpu.make_async_copy(
                        up.at[:, pl.ds(start, block)], store.at[1, :, pl.ds(h * block, block)], sem_half.at[h]
                    )
                )
            return copies

        def swap_copies(do):
            for group, (first, end) in enumerate(live):

                @pl.when((micro >= first) & (micro < end))
                def _():
                    do(to_swap(group))

        swap_copies(lambda copies: [copy.start() for copy in copies[1:]])

        def project(c, carry):
            copy_wo(c).wait()
            datt[:, pl.ds(pl.multiple_of(c * wide, wide), wide)] = nn(up[...], wo[c]).astype(BF)
            return carry

        lax.fori_loop(0, chunks, project, 0)
        if head_major:
            late = [
                pltpu.make_async_copy(
                    datt.at[:, pl.ds(h * slice_w, slice_w)], d_store.at[h, micro], sem_head.at[h]
                )
                for h in range(heads)
            ]
        else:
            late = [pltpu.make_async_copy(datt, d_store.at[micro], sem_head.at[0])]
        for save in late:
            save.start()
        for i in range(span_refs):
            copy_v(i).wait()
        get_probs.wait()
        for i in range(span_refs):
            copy_k(i).wait()

        def one_group(index, carry):
            span, first = index // groups, index % groups * (pairs // groups)
            rws = pl.ds(pl.multiple_of(span * SPAN, SPAN), SPAN)
            for step in range(pairs // groups):
                pair = first + step
                cols = pl.ds(pl.multiple_of(pair * PAIR, PAIR), PAIR)
                val = jnp.concatenate([vb[span * K_NBR + k, :, cols] for k in range(K_NBR)], axis=0)
                key = jnp.concatenate([kb[span * K_NBR + k, :, cols] for k in range(K_NBR)], axis=0)
                d_probs = nt(head_rows(datt[rws, cols]), val)
                prob = pb[span * pairs + pair].astype(F32)
                delta = jnp.sum(prob * d_probs, axis=-1, keepdims=True)
                d_scores = (prob * (d_probs - delta) * SCALE).astype(BF)
                dq[rws, cols] = head_columns(nn(d_scores, key)).astype(BF)
            return carry

        lax.fori_loop(0, spans * groups, one_group, 0)

        swap_copies(lambda copies: copies[0].start())

        def back(c, carry):
            copy_wq(c).wait()
            cols = pl.ds(pl.multiple_of(c * rows, rows), rows)
            gr[:, cols] = (up[:, cols].astype(F32) + nt(dq[...], wq[c])).astype(BF)
            return carry

        lax.fori_loop(0, chunks, back, 0)
        late.append(pltpu.make_async_copy(gr, leaving, sem_out.at[2]))
        late[-1].start()
        late.append(pltpu.make_async_copy(gr, g_store.at[micro], sem_out.at[3]))
        late[-1].start()
        for save in [save_up] + late:
            save.wait()

        swap_copies(lambda copies: [copy.wait() for copy in copies])


def weight_grads_kernel(scale, par, x_own, x_got, up_own, att_own, att_got, *parts_and_out):
    parts, out_ref = parts_and_out[:-1], parts_and_out[-1]
    flat, width = att_own.shape
    output_sum = tn(up_own[...], att_own[...])
    query_sum = 0.0
    row = 0
    for dq_own, dq_got, up_got in zip(parts[::3], parts[1::3], parts[2::3]):
        count = dq_got.shape[0] * dq_got.shape[2]
        rws = slice(row, row + count)
        query_sum += tn(x_own[rws, :], dq_own[...].reshape(count, width))
        query_sum += tn(x_got[rws, :], dq_got[...].reshape(count, width))
        output_sum += tn(up_got[...].reshape(count, up_got.shape[-1]), att_got[rws, :])
        row += count
    out_ref[:, :width] = (query_sum * scale).astype(BF)
    out_ref[:, width:] = (output_sum * scale).astype(BF)


def attended_kernel(scal, values, probs, a0, a_store, vb, pb, att, sem_v, sem_p, sem_a):
    micros, tokens, width = a_store.shape
    spans = tokens // SPAN
    pairs = width // PAIR

    def get_probs(m):
        return pltpu.make_async_copy(probs.at[m], pb.at[m], sem_p.at[m])

    def put(m):
        return pltpu.make_async_copy(att.at[m], a_store.at[m], sem_a.at[m])

    @pl.when(scal[0] > 0)
    def _():
        get_values = pltpu.make_async_copy(values, vb, sem_v)
        get_values.start()
        for m in range(micros):
            get_probs(m).start()
        get_values.wait()

        def one(m, carry):
            get_probs(m).wait()
            for span in range(spans):
                rws = slice(span * SPAN, (span + 1) * SPAN)
                owners = [scal[1 + (m * spans + span) * K_NBR + k] for k in range(K_NBR)]
                for pair in range(pairs):
                    cols = slice(pair * PAIR, (pair + 1) * PAIR)
                    val = jnp.concatenate([vb[o, :, cols] for o in owners], axis=0)
                    att[m, rws, cols] = head_columns(nn(pb[m, span * pairs + pair], val)).astype(BF)
            put(m).start()
            return carry

        lax.fori_loop(0, micros, one, 0)
        for m in range(micros):
            put(m).wait()


def block_grads_kernel(micros, local, ids, mask, q_ref, d_ref, kv_ref, out_ref, acc):
    reader = pl.program_id(0)
    rows, width = d_ref.shape[1], d_ref.shape[2]
    tokens = rows // micros
    spans = tokens // SPAN
    readers = pl.num_programs(0)

    @pl.when(reader == 0)
    def _():
        acc[...] = jnp.zeros_like(acc)

    def block(r, which):
        start = pl.multiple_of((r % local * 2 + which) * NBR_LEN, NBR_LEN)
        return kv_ref[r // local, pl.ds(start, NBR_LEN), :]

    def unit(index, carry):
        at = [((index // spans * readers + reader) * spans + index % spans) * K_NBR + k for k in range(K_NBR)]
        rws = pl.ds(pl.multiple_of(index * SPAN, SPAN), SPAN)
        refs = [ids[i] for i in at]
        keep = [mask[i] > 0 for i in at]
        zero = jnp.zeros((NBR_LEN, width), BF)
        key = jnp.concatenate([jnp.where(m, block(r, 0), zero) for m, r in zip(keep, refs)], axis=0)
        val = jnp.concatenate([jnp.where(m, block(r, 1), zero) for m, r in zip(keep, refs)], axis=0)
        q_rows = head_rows(q_ref[0, rws, :])
        d_rows = head_rows(d_ref[0, rws, :])
        scores = nt(key, q_rows) * SCALE
        weights = jnp.exp(scores - jnp.max(scores, axis=0, keepdims=True))
        prob = weights / jnp.sum(weights, axis=0, keepdims=True)
        d_probs = nt(val, d_rows)
        delta = jnp.sum(prob * d_probs, axis=0, keepdims=True)
        d_scores = (prob * (d_probs - delta) * SCALE).astype(BF)
        d_keys = nn(d_scores, q_rows)
        d_values = nn(prob.astype(BF), d_rows)
        fzero = jnp.zeros((NBR_LEN, width), F32)
        for k in range(K_NBR):
            part = slice(k * NBR_LEN, (k + 1) * NBR_LEN)
            acc[refs[k], 0] += jnp.where(keep[k], d_keys[part], fzero)
            acc[refs[k], 1] += jnp.where(keep[k], d_values[part], fzero)
        return carry

    lax.fori_loop(0, micros * spans, unit, 0, unroll=4)

    @pl.when(reader == readers - 1)
    def _():
        out_ref[...] = acc[...].astype(BF)


def body(
    section_inputs,
    top_grads,
    query_weight,
    output_weight,
    neighbour_kv,
    nbr_ids,
    send_list,
    send_counts,
):
    n_section = lax.axis_size("section")
    section_index = lax.axis_index("section")
    n_data = lax.axis_size("dp")
    data_index = lax.axis_index("dp")
    inputs_all = section_inputs[0]
    w_query = query_weight[0]
    w_out = output_weight[0]
    owned = neighbour_kv[0]
    micros, tokens, model = inputs_all.shape
    blk_dev = owned.shape[0]
    width = w_query.shape[1]
    spans = tokens // SPAN
    slice_w = width // n_data
    params = functools.partial(pltpu.CompilerParams, vmem_limit_bytes=56 << 20)

    near = n_data // 2
    mates = data_index ^ jnp.arange(near, dtype=jnp.int32)

    def wanted(owner):
        row = lax.dynamic_index_in_dim(send_list, owner, 0, keepdims=False)
        counts = lax.dynamic_index_in_dim(send_counts, owner, 0, keepdims=False)
        return jnp.take(row, mates), jnp.take(counts, mates)

    wants = [wanted(data_index), wanted(data_index ^ near)]

    def across(which, behind):
        own = owned[:, which]
        if behind is not None:
            own, behind = lax.optimization_barrier((own, behind))
        return own, lax.ppermute(own, "dp", [(i, i ^ near) for i in range(n_data)])

    def picked(copies):
        pieces = []
        for k in range(near):
            piece = []
            for blocks, (which_block, counts) in zip(copies, wants):
                chosen = jnp.zeros((NBR_LEN, width), BF)
                for b in range(blk_dev):
                    chosen = jnp.where((which_block[k] == b) & (counts[k] > 0), blocks[b], chosen)
                piece.append(chosen)
            pieces.append(jnp.stack(piece))
        return pieces

    def fetch(pieces):
        moved = [lax.ppermute(pieces[k], "dp", [(i, i ^ k) for i in range(n_data)]) for k in range(1, near)]
        return jnp.concatenate(pieces[:1] + moved, axis=0)

    def exchange(x):
        return lax.all_to_all(x, "dp", split_axis=0, concat_axis=0, tiled=True)

    key_copies = across(0, None)
    value_copies = across(1, key_copies[1])
    key_pieces, inputs_all = lax.optimization_barrier((picked(key_copies), inputs_all))
    keys = fetch(key_pieces)
    query = nn(inputs_all.reshape(micros * tokens, model), w_query).astype(BF)
    held = lax.optimization_barrier((picked(value_copies), query, inputs_all, owned, nbr_ids))
    value_pieces, query, inputs_all, owned, nbr_ids = held
    values = fetch(value_pieces)
    query = query.reshape(micros, tokens, width)
    apart = (nbr_ids // blk_dev).astype(jnp.int32) ^ data_index
    owners = apart % near * 2 + apart // near

    probs = pl.pallas_call(
        probs_kernel,
        cost_estimate=cost(7),
        out_shape=jax.ShapeDtypeStruct((micros, spans * width // PAIR, 2 * SPAN, KEYS), BF),
        grid_spec=pltpu.PrefetchScalarGridSpec(
            num_scalar_prefetch=1,
            grid=(micros,),
            in_specs=[
                pl.BlockSpec((1, tokens, width), lambda i, o: (i, 0, 0)),
                pl.BlockSpec((n_data, NBR_LEN, width), lambda i, o: (0, 0, 0)),
            ],
            out_specs=pl.BlockSpec((1, spans * width // PAIR, 2 * SPAN, KEYS), lambda i, o: (i, 0, 0, 0)),
        ),
        compiler_params=params(),
    )(owners.reshape(-1), query, keys)

    def by_heads(x):
        return jnp.moveaxis(x.reshape(-1, n_data, slice_w), 1, 0)

    q_rows = micros * tokens
    kv_rows = blk_dev * 2 * NBR_LEN
    id_rows = micros * spans * K_NBR
    id_tile = jnp.broadcast_to(nbr_ids.reshape(1, id_rows, 1).astype(BF), (n_data, id_rows, slice_w))
    sliced = jnp.concatenate([by_heads(query), by_heads(owned), id_tile], axis=1)

    partners = [(i, i ^ 1) for i in range(n_data)]
    parity = data_index % 2
    flat = micros * tokens
    halves = n_data // 2
    half = model // 2
    block = model // n_data

    def swap(x):
        return lax.ppermute(x, "dp", partners)

    flat_in = inputs_all.reshape(flat, model)
    inputs_other = jnp.concatenate(
        [lax.dynamic_slice_in_dim(flat_in, (2 * h + 1 - parity) * block, block, axis=1) for h in range(halves)],
        axis=1,
    )

    chunks = 4
    ticks = micros + 2 * (n_section - 1)
    refs = spans * K_NBR
    micro_at = jnp.arange(ticks, dtype=jnp.int32) - 2 * (n_section - 1 - section_index)
    slot_at = jnp.clip(micro_at, 0, micros - 1)
    is_last = (section_index == n_section - 1).astype(jnp.int32)
    other = (1 - parity).astype(jnp.int32)
    table = jnp.concatenate(
        [
            slot_at[:, None],
            ((micro_at >= 0) & (micro_at < micros)).astype(jnp.int32)[:, None],
            jnp.broadcast_to(jnp.stack([is_last, other]), (ticks, 2)),
            jnp.take(owners.reshape(micros, refs), slot_at, axis=0),
        ],
        axis=1,
    ).astype(jnp.int32)
    scal = table.reshape(-1)
    head_major = slice_w % 128 == 0
    d_shape = (n_data, micros, tokens, slice_w) if head_major else (micros, tokens, width)
    swap_groups = [(micros - 1, micros), (micros - 2, micros - 1), (0, micros - 2)]
    store_shapes = (
        jax.ShapeDtypeStruct((micros, tokens, model), BF),
        jax.ShapeDtypeStruct((micros, tokens, model), BF),
        jax.ShapeDtypeStruct(d_shape, BF),
        *(jax.ShapeDtypeStruct((end - first, 2, tokens, width), BF) for first, end in swap_groups),
    )

    def tick(index, arriving, stores):
        live = [group for group in swap_groups if ticks - micros + group[1] > index]
        count = 3 + len(live)
        out = pl.pallas_call(
            functools.partial(tick_kernel, chunks, index * table.shape[1], head_major, live),
            out_shape=(jax.ShapeDtypeStruct((tokens, model), BF), *store_shapes[:count]),
            in_specs=[pl.BlockSpec(memory_space=pltpu.SMEM)] + [ANY] * (7 + count),
            out_specs=[ANY] * (1 + count),
            scratch_shapes=[
                pltpu.VMEM((tokens, model), BF),
                pltpu.VMEM((chunks, model, width // chunks), BF),
                pltpu.VMEM((chunks, model // chunks, width), BF),
                pltpu.VMEM((refs, NBR_LEN, width), BF),
                pltpu.VMEM((refs, NBR_LEN, width), BF),
                pltpu.VMEM((spans * width // PAIR, 2 * SPAN, KEYS), BF),
                pltpu.VMEM((tokens, width), BF),
                pltpu.VMEM((tokens, width), BF),
                pltpu.VMEM((tokens, model), BF),
                pltpu.SemaphoreType.DMA,
                pltpu.SemaphoreType.DMA((chunks,)),
                pltpu.SemaphoreType.DMA((chunks,)),
                pltpu.SemaphoreType.DMA((refs,)),
                pltpu.SemaphoreType.DMA((refs,)),
                pltpu.SemaphoreType.DMA,
                pltpu.SemaphoreType.DMA((4,)),
                pltpu.SemaphoreType.DMA((halves,)),
                pltpu.SemaphoreType.DMA((n_data if head_major else 1,)),
            ],
            input_output_aliases={8 + i: 1 + i for i in range(count)},
            cost_estimate=cost(11),
            compiler_params=params(),
        )(scal, arriving, top_grads, w_out, w_query, keys, values, probs, *stores[:count])
        return (*out, *stores[count:])

    def unwritten(*shapes):
        return pl.pallas_call(
            lambda *refs: None,
            out_shape=shapes,
            out_specs=[ANY] * len(shapes),
        )()

    def attend(enabled, store):
        return pl.pallas_call(
            attended_kernel,
            out_shape=jax.ShapeDtypeStruct((micros, tokens, width), BF),
            grid_spec=pltpu.PrefetchScalarGridSpec(
                num_scalar_prefetch=1,
                grid=(1,),
                in_specs=[ANY] * 3,
                out_specs=ANY,
                scratch_shapes=[
                    pltpu.VMEM((n_data, NBR_LEN, width), BF),
                    pltpu.VMEM((micros, spans * width // PAIR, 2 * SPAN, KEYS), BF),
                    pltpu.VMEM((micros, tokens, width), BF),
                    pltpu.SemaphoreType.DMA,
                    pltpu.SemaphoreType.DMA((micros,)),
                    pltpu.SemaphoreType.DMA((micros,)),
                ],
            ),
            input_output_aliases={3: 0},
            cost_estimate=cost(5),
            compiler_params=params(),
        )(jnp.concatenate([enabled[None].astype(jnp.int32), owners.reshape(-1)]), values, probs, store)

    *stores, attended = unwritten(*store_shapes, jax.ShapeDtypeStruct((micros, tokens, width), BF))
    arrived = [jnp.zeros((tokens, model), BF)] * 2
    got = []
    for index in range(ticks):
        if index == micros + 3:
            arrived[index], attended_got = lax.optimization_barrier((arrived[index], attended_got))
        leaving, *stores = tick(index, arrived[index], stores)
        if index == 0:
            sliced, inputs_other, leaving, attended = lax.optimization_barrier((sliced, inputs_other, leaving, attended))
            sliced = exchange(sliced)
            inputs_got = swap(inputs_other)
            attended = attend(1 - is_last, attended)
            stores[0], attended = lax.optimization_barrier((stores[0], attended))
        hops = []
        for s in range(1, n_section):
            if 0 <= index - 2 * (n_section - 1 - s) < micros:
                hops.append((s, s - 1))
        if index > 0:
            held = lax.optimization_barrier((leaving, arrived[index + 1]))
            if hops:
                leaving, arrived[index + 1] = held
        arrived.append(lax.ppermute(leaving, "section", hops) if hops else leaving)
        if index == micros:
            attended = attend(is_last, attended)
            stores[0], attended = lax.optimization_barrier((stores[0], attended))
            held = lax.optimization_barrier((arrived[index + 1], sliced, inputs_got))
            arrived[index + 1], sliced, inputs_got = held
            attended_got = swap(attended.reshape(flat, width))
        for group, (_, end) in enumerate(swap_groups):
            if end == index - (ticks - micros) + 1:
                at = 3 + group
                if hops:
                    stores[at], arrived[index + 1] = lax.optimization_barrier((stores[at], arrived[index + 1]))
                if group == 0:
                    stores[at], stores[2], got = lax.optimization_barrier((stores[at], stores[2], got))
                got.append(swap(stores[at]))
    grads_in, upstream, d_store, *s_stores = stores

    grad_scale = (flat * n_data) ** (-0.5)
    parts = []
    part_specs = []
    for own, part in zip(s_stores[::-1], got):
        count = part.shape[0]
        parts += [own, part, part]
        part_specs += [
            pl.BlockSpec((count, 1, tokens, width), lambda j, p: (0, 0, 0, 0)),
            pl.BlockSpec((count, 1, tokens, width), lambda j, p: (0, 0, 0, 0)),
            pl.BlockSpec((count, 1, tokens, block), lambda j, p: (0, 1, 0, j)),
        ]
    terms = pl.pallas_call(
        functools.partial(weight_grads_kernel, grad_scale),
        cost_estimate=cost(9),
        out_shape=jax.ShapeDtypeStruct((half, 2 * width), BF),
        grid_spec=pltpu.PrefetchScalarGridSpec(
            num_scalar_prefetch=1,
            grid=(halves,),
            in_specs=[
                pl.BlockSpec((flat, block), lambda j, p: (0, 2 * j + p[0])),
                pl.BlockSpec((flat, block), lambda j, p: (0, j)),
                pl.BlockSpec((flat, block), lambda j, p: (0, 2 * j + p[0])),
                pl.BlockSpec((flat, width), lambda j, p: (0, 0)),
                pl.BlockSpec((flat, width), lambda j, p: (0, 0)),
                *part_specs,
            ],
            out_specs=pl.BlockSpec((block, 2 * width), lambda j, p: (j, 0)),
        ),
        compiler_params=params(),
    )(
        parity[None].astype(jnp.int32),
        inputs_all.reshape(flat, model),
        inputs_got,
        upstream.reshape(flat, model),
        attended.reshape(flat, width),
        attended_got,
        *parts,
    )
    d_heads = exchange(d_store) if head_major else exchange(by_heads(d_store))
    d_heads = d_heads.reshape(n_data, q_rows, slice_w)
    terms, d_heads = lax.optimization_barrier((terms, d_heads))
    shares = lax.psum_scatter(
        terms,
        "dp",
        scatter_dimension=0,
        tiled=True,
        axis_index_groups=[list(range(p, n_data, 2)) for p in range(2)],
    )

    ids_all = sliced[:, q_rows + kv_rows :, 0].astype(jnp.int32).reshape(n_data, micros, spans, K_NBR)
    ids_all = jnp.moveaxis(ids_all, 0, 1).reshape(micros, n_data * spans, K_NBR)
    owner_all = ids_all // blk_dev
    reader_all = (jnp.arange(n_data * spans, dtype=jnp.int32) // spans)[None, :, None]
    hit_owner = owner_all[..., None] == jnp.arange(n_data, dtype=jnp.int32)
    list_r = jnp.take(send_list, reader_all[0, :, 0], axis=1).T[None, :, None, :]
    count_r = jnp.take(send_counts, reader_all[0, :, 0], axis=1).T[None, :, None, :]
    block_all = owner_all * blk_dev + jnp.sum(jnp.where(hit_owner, list_r, 0), axis=-1)
    mask_all = jnp.sum(jnp.where(hit_owner, count_r, 0), axis=-1)
    blocks = n_data * blk_dev
    block_grads = pl.pallas_call(
        functools.partial(block_grads_kernel, micros, blk_dev),
        cost_estimate=cost(37),
        out_shape=jax.ShapeDtypeStruct((blocks, 2, NBR_LEN, slice_w), BF),
        grid_spec=pltpu.PrefetchScalarGridSpec(
            num_scalar_prefetch=2,
            grid=(n_data,),
            in_specs=[
                pl.BlockSpec((1, q_rows, slice_w), lambda i, a, b: (i, 0, 0)),
                pl.BlockSpec((1, q_rows, slice_w), lambda i, a, b: (i, 0, 0)),
                pl.BlockSpec((n_data, kv_rows, slice_w), lambda i, a, b: (0, q_rows // kv_rows, 0)),
            ],
            out_specs=pl.BlockSpec((blocks, 2, NBR_LEN, slice_w), lambda i, a, b: (0, 0, 0, 0)),
            scratch_shapes=[pltpu.VMEM((blocks, 2, NBR_LEN, slice_w), F32)],
        ),
        compiler_params=params(),
    )(block_all.reshape(-1).astype(jnp.int32), mask_all.reshape(-1).astype(jnp.int32), sliced, d_heads, sliced)
    returned = exchange(block_grads.reshape(n_data, blk_dev, 2, NBR_LEN, slice_w))
    kv_grads = jnp.moveaxis(returned, 0, -2).reshape(blk_dev, 2, NBR_LEN, width)
    return (
        grads_in[None],
        shares[None, :, :width],
        shares[None, :, width:],
        kv_grads[None],
    )


def solution(mesh):
    in_specs = (
        P("section", None, "dp", None),
        P(None, "dp", None),
        P("section", None, None),
        P("section", None, None),
        P("section", "dp", None, None, None),
        P(None, "dp", None),
        P(),
        P(),
    )
    out_specs = (
        P("section", None, "dp", None),
        P("section", "dp", None),
        P("section", "dp", None),
        P("section", "dp", None, None, None),
    )
    return jax.shard_map(body, mesh=mesh, in_specs=in_specs, out_specs=out_specs, check_vma=False)
```

```python
import functools

import jax
import jax.numpy as jnp
from jax import lax
from jax.experimental import pallas as pl
from jax.experimental.pallas import tpu as pltpu
from jax.sharding import PartitionSpec as P

HEADS = 16
HEAD_DIM = 64
SPAN = 64
K_NBR = 2
NBR_LEN = 128
PAIR = 2 * HEAD_DIM
KEYS = K_NBR * NBR_LEN
SCALE = HEAD_DIM ** (-0.5)
BF = jnp.bfloat16
F32 = jnp.float32
ANY = pl.BlockSpec(memory_space=pl.ANY)


def cost(micros_of_work):
    return pl.CostEstimate(flops=0, transcendentals=0, bytes_accessed=int(micros_of_work * 3.6e6))


def nt(a, b):
    return lax.dot_general(a, b, (((1,), (1,)), ((), ())), preferred_element_type=F32)


def nn(a, b):
    return lax.dot_general(a, b, (((1,), (0,)), ((), ())), preferred_element_type=F32)


def tn(a, b):
    return lax.dot_general(a, b, (((0,), (0,)), ((), ())), preferred_element_type=F32)


def head_rows(x):
    heads = x.shape[1] // HEAD_DIM
    if heads == 1:
        return x
    lane = lax.broadcasted_iota(jnp.int32, x.shape, 1) // HEAD_DIM
    zero = jnp.zeros_like(x)
    return jnp.concatenate([jnp.where(lane == h, x, zero) for h in range(heads)], axis=0)


def head_columns(y):
    heads = y.shape[1] // HEAD_DIM
    out = y[:SPAN]
    lane = lax.broadcasted_iota(jnp.int32, out.shape, 1) // HEAD_DIM
    for h in range(1, heads):
        out = jnp.where(lane == h, y[h * SPAN : (h + 1) * SPAN], out)
    return out


def softmax_rows(scores):
    weights = jnp.exp(scores - jnp.max(scores, axis=-1, keepdims=True))
    return weights / jnp.sum(weights, axis=-1, keepdims=True)


def probs_kernel(owners, q_ref, k_ref, out_ref):
    micro = pl.program_id(0)
    tokens, width = q_ref.shape[1], q_ref.shape[2]
    spans = tokens // SPAN
    for span in range(spans):
        refs = [owners[(micro * spans + span) * K_NBR + k] for k in range(K_NBR)]
        for pair in range(width // PAIR):
            cols = slice(pair * PAIR, (pair + 1) * PAIR)
            keys = jnp.concatenate([k_ref[r, :, cols] for r in refs], axis=0)
            rows = head_rows(q_ref[0, span * SPAN : (span + 1) * SPAN, cols])
            out_ref[0, span * (width // PAIR) + pair] = softmax_rows(nt(rows, keys) * SCALE).astype(BF)


def tick_kernel(
    chunks, base, head_major, live,
    scal,
    arriving, top, w_out, w_query, keys, values, probs,
    *refs,
):
    count = 3 + len(live)
    leaving, g_store, u_store, d_store, *s_stores = refs[count : 2 * count + 1]
    (
        up, wo, wq, kb, vb, pb, datt, dq, gr,
        sem_up, sem_wo, sem_wq, sem_k, sem_v, sem_p, sem_out, sem_half, sem_head,
    ) = refs[2 * count + 1 :]
    micro = scal[base]
    valid = scal[base + 1]
    last = scal[base + 2]
    other = scal[base + 3]
    tokens, model = up.shape
    width = datt.shape[1]
    spans = tokens // SPAN
    span_refs = spans * K_NBR
    pairs = width // PAIR
    rows = model // chunks
    wide = width // chunks
    groups = 1
    halves = sem_half.shape[0]
    block = model // (2 * halves)
    heads = sem_head.shape[0]
    slice_w = width // heads

    def copy_wo(c):
        return pltpu.make_async_copy(w_out.at[:, pl.ds(c * wide, wide)], wo.at[c], sem_wo.at[c])

    def copy_wq(c):
        return pltpu.make_async_copy(w_query.at[pl.ds(c * rows, rows)], wq.at[c], sem_wq.at[c])

    def copy_v(i):
        return pltpu.make_async_copy(values.at[scal[base + 4 + i]], vb.at[i], sem_v.at[i])

    def copy_k(i):
        return pltpu.make_async_copy(keys.at[scal[base + 4 + i]], kb.at[i], sem_k.at[i])

    @pl.when(valid > 0)
    def _():
        from_top = pltpu.make_async_copy(top.at[micro], up, sem_up)
        from_hop = pltpu.make_async_copy(arriving, up, sem_up)

        @pl.when(last > 0)
        def _():
            from_top.start()

        @pl.when(last == 0)
        def _():
            from_hop.start()

        for c in range(chunks):
            copy_wo(c).start()
        for i in range(span_refs):
            copy_v(i).start()
        get_probs = pltpu.make_async_copy(probs.at[micro], pb, sem_p)
        get_probs.start()
        for i in range(span_refs):
            copy_k(i).start()
        for c in range(chunks):
            copy_wq(c).start()

        from_hop.wait()
        save_up = pltpu.make_async_copy(up, u_store.at[micro], sem_out.at[0])
        save_up.start()
        def to_swap(group):
            store = s_stores[group].at[micro - live[group][0]]
            copies = [pltpu.make_async_copy(dq, store.at[0], sem_out.at[1])]
            for h in range(halves):
                start = pl.multiple_of((2 * h + other) * block, block)
                copies.append(
                    pltpu.make_async_copy(
                        up.at[:, pl.ds(start, block)], store.at[1, :, pl.ds(h * block, block)], sem_half.at[h]
                    )
                )
            return copies

        def swap_copies(do):
            for group, (first, end) in enumerate(live):

                @pl.when((micro >= first) & (micro < end))
                def _():
                    do(to_swap(group))

        swap_copies(lambda copies: [copy.start() for copy in copies[1:]])

        def project(c, carry):
            copy_wo(c).wait()
            datt[:, pl.ds(pl.multiple_of(c * wide, wide), wide)] = nn(up[...], wo[c]).astype(BF)
            return carry

        lax.fori_loop(0, chunks, project, 0)
        if head_major:
            late = [
                pltpu.make_async_copy(
                    datt.at[:, pl.ds(h * slice_w, slice_w)], d_store.at[h, micro], sem_head.at[h]
                )
                for h in range(heads)
            ]
        else:
            late = [pltpu.make_async_copy(datt, d_store.at[micro], sem_head.at[0])]
        for save in late:
            save.start()
        for i in range(span_refs):
            copy_v(i).wait()
        get_probs.wait()
        for i in range(span_refs):
            copy_k(i).wait()

        def one_group(index, carry):
            span, first = index // groups, index % groups * (pairs // groups)
            rws = pl.ds(pl.multiple_of(span * SPAN, SPAN), SPAN)
            for step in range(pairs // groups):
                pair = first + step
                cols = pl.ds(pl.multiple_of(pair * PAIR, PAIR), PAIR)
                val = jnp.concatenate([vb[span * K_NBR + k, :, cols] for k in range(K_NBR)], axis=0)
                key = jnp.concatenate([kb[span * K_NBR + k, :, cols] for k in range(K_NBR)], axis=0)
                d_probs = nt(head_rows(datt[rws, cols]), val)
                prob = pb[span * pairs + pair].astype(F32)
                delta = jnp.sum(prob * d_probs, axis=-1, keepdims=True)
                d_scores = (prob * (d_probs - delta) * SCALE).astype(BF)
                dq[rws, cols] = head_columns(nn(d_scores, key)).astype(BF)
            return carry

        lax.fori_loop(0, spans * groups, one_group, 0)

        swap_copies(lambda copies: copies[0].start())

        def back(c, carry):
            copy_wq(c).wait()
            cols = pl.ds(pl.multiple_of(c * rows, rows), rows)
            gr[:, cols] = (up[:, cols].astype(F32) + nt(dq[...], wq[c])).astype(BF)
            return carry

        lax.fori_loop(0, chunks, back, 0)
        late.append(pltpu.make_async_copy(gr, leaving, sem_out.at[2]))
        late[-1].start()
        late.append(pltpu.make_async_copy(gr, g_store.at[micro], sem_out.at[3]))
        late[-1].start()
        for save in [save_up] + late:
            save.wait()

        swap_copies(lambda copies: [copy.wait() for copy in copies])


def weight_grads_kernel(scale, par, x_own, x_got, up_own, att_own, att_got, *parts_and_out):
    parts, out_ref = parts_and_out[:-1], parts_and_out[-1]
    flat, width = att_own.shape
    output_sum = tn(up_own[...], att_own[...])
    query_sum = 0.0
    row = 0
    for dq_own, dq_got, up_got in zip(parts[::3], parts[1::3], parts[2::3]):
        count = dq_got.shape[0] * dq_got.shape[2]
        rws = slice(row, row + count)
        query_sum += tn(x_own[rws, :], dq_own[...].reshape(count, width))
        query_sum += tn(x_got[rws, :], dq_got[...].reshape(count, width))
        output_sum += tn(up_got[...].reshape(count, up_got.shape[-1]), att_got[rws, :])
        row += count
    out_ref[:, :width] = (query_sum * scale).astype(BF)
    out_ref[:, width:] = (output_sum * scale).astype(BF)


def attended_kernel(scal, values, probs, a0, a_store, vb, pb, att, sem_v, sem_p, sem_a):
    micros, tokens, width = a_store.shape
    spans = tokens // SPAN
    pairs = width // PAIR

    def get_probs(m):
        return pltpu.make_async_copy(probs.at[m], pb.at[m], sem_p.at[m])

    def put(m):
        return pltpu.make_async_copy(att.at[m], a_store.at[m], sem_a.at[m])

    @pl.when(scal[0] > 0)
    def _():
        get_values = pltpu.make_async_copy(values, vb, sem_v)
        get_values.start()
        for m in range(micros):
            get_probs(m).start()
        get_values.wait()

        def one(m, carry):
            get_probs(m).wait()
            for span in range(spans):
                rws = slice(span * SPAN, (span + 1) * SPAN)
                owners = [scal[1 + (m * spans + span) * K_NBR + k] for k in range(K_NBR)]
                for pair in range(pairs):
                    cols = slice(pair * PAIR, (pair + 1) * PAIR)
                    val = jnp.concatenate([vb[o, :, cols] for o in owners], axis=0)
                    att[m, rws, cols] = head_columns(nn(pb[m, span * pairs + pair], val)).astype(BF)
            put(m).start()
            return carry

        lax.fori_loop(0, micros, one, 0)
        for m in range(micros):
            put(m).wait()


def block_grads_kernel(micros, local, ids, mask, q_ref, d_ref, kv_ref, out_ref, acc):
    reader = pl.program_id(0)
    rows, width = d_ref.shape[1], d_ref.shape[2]
    tokens = rows // micros
    spans = tokens // SPAN
    readers = pl.num_programs(0)

    @pl.when(reader == 0)
    def _():
        acc[...] = jnp.zeros_like(acc)

    def block(r, which):
        start = pl.multiple_of((r % local * 2 + which) * NBR_LEN, NBR_LEN)
        return kv_ref[r // local, pl.ds(start, NBR_LEN), :]

    def unit(index, carry):
        at = [((index // spans * readers + reader) * spans + index % spans) * K_NBR + k for k in range(K_NBR)]
        rws = pl.ds(pl.multiple_of(index * SPAN, SPAN), SPAN)
        refs = [ids[i] for i in at]
        keep = [mask[i] > 0 for i in at]
        zero = jnp.zeros((NBR_LEN, width), BF)
        key = jnp.concatenate([jnp.where(m, block(r, 0), zero) for m, r in zip(keep, refs)], axis=0)
        val = jnp.concatenate([jnp.where(m, block(r, 1), zero) for m, r in zip(keep, refs)], axis=0)
        q_rows = head_rows(q_ref[0, rws, :])
        d_rows = head_rows(d_ref[0, rws, :])
        scores = nt(key, q_rows) * SCALE
        weights = jnp.exp(scores - jnp.max(scores, axis=0, keepdims=True))
        prob = weights / jnp.sum(weights, axis=0, keepdims=True)
        d_probs = nt(val, d_rows)
        delta = jnp.sum(prob * d_probs, axis=0, keepdims=True)
        d_scores = (prob * (d_probs - delta) * SCALE).astype(BF)
        d_keys = nn(d_scores, q_rows)
        d_values = nn(prob.astype(BF), d_rows)
        fzero = jnp.zeros((NBR_LEN, width), F32)
        for k in range(K_NBR):
            part = slice(k * NBR_LEN, (k + 1) * NBR_LEN)
            acc[refs[k], 0] += jnp.where(keep[k], d_keys[part], fzero)
            acc[refs[k], 1] += jnp.where(keep[k], d_values[part], fzero)
        return carry

    lax.fori_loop(0, micros * spans, unit, 0, unroll=4)

    @pl.when(reader == readers - 1)
    def _():
        out_ref[...] = acc[...].astype(BF)


def body(
    section_inputs,
    top_grads,
    query_weight,
    output_weight,
    neighbour_kv,
    nbr_ids,
    send_list,
    send_counts,
):
    n_section = lax.axis_size("section")
    section_index = lax.axis_index("section")
    n_data = lax.axis_size("dp")
    data_index = lax.axis_index("dp")
    inputs_all = section_inputs[0]
    w_query = query_weight[0]
    w_out = output_weight[0]
    owned = neighbour_kv[0]
    micros, tokens, model = inputs_all.shape
    blk_dev = owned.shape[0]
    width = w_query.shape[1]
    spans = tokens // SPAN
    slice_w = width // n_data
    params = functools.partial(pltpu.CompilerParams, vmem_limit_bytes=56 << 20)

    near = n_data // 2
    mates = data_index ^ jnp.arange(near, dtype=jnp.int32)

    def wanted(owner):
        row = lax.dynamic_index_in_dim(send_list, owner, 0, keepdims=False)
        counts = lax.dynamic_index_in_dim(send_counts, owner, 0, keepdims=False)
        return jnp.take(row, mates), jnp.take(counts, mates)

    wants = [wanted(data_index), wanted(data_index ^ near)]

    def across(which, behind):
        own = owned[:, which]
        if behind is not None:
            own, behind = lax.optimization_barrier((own, behind))
        return own, lax.ppermute(own, "dp", [(i, i ^ near) for i in range(n_data)])

    def picked(copies):
        pieces = []
        for k in range(near):
            piece = []
            for blocks, (which_block, counts) in zip(copies, wants):
                chosen = jnp.zeros((NBR_LEN, width), BF)
                for b in range(blk_dev):
                    chosen = jnp.where((which_block[k] == b) & (counts[k] > 0), blocks[b], chosen)
                piece.append(chosen)
            pieces.append(jnp.stack(piece))
        return pieces

    def fetch(pieces):
        moved = [lax.ppermute(pieces[k], "dp", [(i, i ^ k) for i in range(n_data)]) for k in range(1, near)]
        return jnp.concatenate(pieces[:1] + moved, axis=0)

    def exchange(x):
        return lax.all_to_all(x, "dp", split_axis=0, concat_axis=0, tiled=True)

    key_copies = across(0, None)
    value_copies = across(1, key_copies[1])
    key_pieces, inputs_all = lax.optimization_barrier((picked(key_copies), inputs_all))
    keys = fetch(key_pieces)
    query = nn(inputs_all.reshape(micros * tokens, model), w_query).astype(BF)
    held = lax.optimization_barrier((picked(value_copies), query, inputs_all, owned, nbr_ids))
    value_pieces, query, inputs_all, owned, nbr_ids = held
    values = fetch(value_pieces)
    query = query.reshape(micros, tokens, width)
    apart = (nbr_ids // blk_dev).astype(jnp.int32) ^ data_index
    owners = apart % near * 2 + apart // near

    probs = pl.pallas_call(
        probs_kernel,
        cost_estimate=cost(7),
        out_shape=jax.ShapeDtypeStruct((micros, spans * width // PAIR, 2 * SPAN, KEYS), BF),
        grid_spec=pltpu.PrefetchScalarGridSpec(
            num_scalar_prefetch=1,
            grid=(micros,),
            in_specs=[
                pl.BlockSpec((1, tokens, width), lambda i, o: (i, 0, 0)),
                pl.BlockSpec((n_data, NBR_LEN, width), lambda i, o: (0, 0, 0)),
            ],
            out_specs=pl.BlockSpec((1, spans * width // PAIR, 2 * SPAN, KEYS), lambda i, o: (i, 0, 0, 0)),
        ),
        compiler_params=params(),
    )(owners.reshape(-1), query, keys)

    def by_heads(x):
        return jnp.moveaxis(x.reshape(-1, n_data, slice_w), 1, 0)

    q_rows = micros * tokens
    kv_rows = blk_dev * 2 * NBR_LEN
    id_rows = micros * spans * K_NBR
    id_tile = jnp.broadcast_to(nbr_ids.reshape(1, id_rows, 1).astype(BF), (n_data, id_rows, slice_w))
    sliced = jnp.concatenate([by_heads(query), by_heads(owned), id_tile], axis=1)

    partners = [(i, i ^ 1) for i in range(n_data)]
    parity = data_index % 2
    flat = micros * tokens
    halves = n_data // 2
    half = model // 2
    block = model // n_data

    def swap(x):
        return lax.ppermute(x, "dp", partners)

    flat_in = inputs_all.reshape(flat, model)
    inputs_other = jnp.concatenate(
        [lax.dynamic_slice_in_dim(flat_in, (2 * h + 1 - parity) * block, block, axis=1) for h in range(halves)],
        axis=1,
    )

    chunks = 4
    ticks = micros + 2 * (n_section - 1)
    refs = spans * K_NBR
    micro_at = jnp.arange(ticks, dtype=jnp.int32) - 2 * (n_section - 1 - section_index)
    slot_at = jnp.clip(micro_at, 0, micros - 1)
    is_last = (section_index == n_section - 1).astype(jnp.int32)
    other = (1 - parity).astype(jnp.int32)
    table = jnp.concatenate(
        [
            slot_at[:, None],
            ((micro_at >= 0) & (micro_at < micros)).astype(jnp.int32)[:, None],
            jnp.broadcast_to(jnp.stack([is_last, other]), (ticks, 2)),
            jnp.take(owners.reshape(micros, refs), slot_at, axis=0),
        ],
        axis=1,
    ).astype(jnp.int32)
    scal = table.reshape(-1)
    head_major = slice_w % 128 == 0
    d_shape = (n_data, micros, tokens, slice_w) if head_major else (micros, tokens, width)
    swap_groups = [(micros - 1, micros), (micros - 2, micros - 1), (0, micros - 2)]
    store_shapes = (
        jax.ShapeDtypeStruct((micros, tokens, model), BF),
        jax.ShapeDtypeStruct((micros, tokens, model), BF),
        jax.ShapeDtypeStruct(d_shape, BF),
        *(jax.ShapeDtypeStruct((end - first, 2, tokens, width), BF) for first, end in swap_groups),
    )

    def tick(index, arriving, stores):
        live = [group for group in swap_groups if ticks - micros + group[1] > index]
        count = 3 + len(live)
        out = pl.pallas_call(
            functools.partial(tick_kernel, chunks, index * table.shape[1], head_major, live),
            out_shape=(jax.ShapeDtypeStruct((tokens, model), BF), *store_shapes[:count]),
            in_specs=[pl.BlockSpec(memory_space=pltpu.SMEM)] + [ANY] * (7 + count),
            out_specs=[ANY] * (1 + count),
            scratch_shapes=[
                pltpu.VMEM((tokens, model), BF),
                pltpu.VMEM((chunks, model, width // chunks), BF),
                pltpu.VMEM((chunks, model // chunks, width), BF),
                pltpu.VMEM((refs, NBR_LEN, width), BF),
                pltpu.VMEM((refs, NBR_LEN, width), BF),
                pltpu.VMEM((spans * width // PAIR, 2 * SPAN, KEYS), BF),
                pltpu.VMEM((tokens, width), BF),
                pltpu.VMEM((tokens, width), BF),
                pltpu.VMEM((tokens, model), BF),
                pltpu.SemaphoreType.DMA,
                pltpu.SemaphoreType.DMA((chunks,)),
                pltpu.SemaphoreType.DMA((chunks,)),
                pltpu.SemaphoreType.DMA((refs,)),
                pltpu.SemaphoreType.DMA((refs,)),
                pltpu.SemaphoreType.DMA,
                pltpu.SemaphoreType.DMA((4,)),
                pltpu.SemaphoreType.DMA((halves,)),
                pltpu.SemaphoreType.DMA((n_data if head_major else 1,)),
            ],
            input_output_aliases={8 + i: 1 + i for i in range(count)},
            cost_estimate=cost(11),
            compiler_params=params(),
        )(scal, arriving, top_grads, w_out, w_query, keys, values, probs, *stores[:count])
        return (*out, *stores[count:])

    def unwritten(*shapes):
        return pl.pallas_call(
            lambda *refs: None,
            out_shape=shapes,
            out_specs=[ANY] * len(shapes),
        )()

    def attend(enabled, store):
        return pl.pallas_call(
            attended_kernel,
            out_shape=jax.ShapeDtypeStruct((micros, tokens, width), BF),
            grid_spec=pltpu.PrefetchScalarGridSpec(
                num_scalar_prefetch=1,
                grid=(1,),
                in_specs=[ANY] * 3,
                out_specs=ANY,
                scratch_shapes=[
                    pltpu.VMEM((n_data, NBR_LEN, width), BF),
                    pltpu.VMEM((micros, spans * width // PAIR, 2 * SPAN, KEYS), BF),
                    pltpu.VMEM((micros, tokens, width), BF),
                    pltpu.SemaphoreType.DMA,
                    pltpu.SemaphoreType.DMA((micros,)),
                    pltpu.SemaphoreType.DMA((micros,)),
                ],
            ),
            input_output_aliases={3: 0},
            cost_estimate=cost(5),
            compiler_params=params(),
        )(jnp.concatenate([enabled[None].astype(jnp.int32), owners.reshape(-1)]), values, probs, store)

    *stores, attended, no_arrival = unwritten(
        *store_shapes,
        jax.ShapeDtypeStruct((micros, tokens, width), BF),
        jax.ShapeDtypeStruct((tokens, model), BF),
    )
    arrived = [no_arrival] * 2
    got = []
    for index in range(ticks):
        if index == micros + 3:
            arrived[index], attended_got = lax.optimization_barrier((arrived[index], attended_got))
        leaving, *stores = tick(index, arrived[index], stores)
        if index == 0:
            sliced, inputs_other, leaving, attended = lax.optimization_barrier((sliced, inputs_other, leaving, attended))
            sliced = exchange(sliced)
            inputs_got = swap(inputs_other)
            attended = attend(1 - is_last, attended)
            stores[0], attended = lax.optimization_barrier((stores[0], attended))
        hops = []
        for s in range(1, n_section):
            if 0 <= index - 2 * (n_section - 1 - s) < micros:
                hops.append((s, s - 1))
        if index > 0:
            held = lax.optimization_barrier((leaving, arrived[index + 1]))
            if hops:
                leaving, arrived[index + 1] = held
        arrived.append(lax.ppermute(leaving, "section", hops) if hops else leaving)
        if index == micros:
            attended = attend(is_last, attended)
            stores[0], attended = lax.optimization_barrier((stores[0], attended))
            held = lax.optimization_barrier((arrived[index + 1], sliced, inputs_got))
            arrived[index + 1], sliced, inputs_got = held
            attended_got = swap(attended.reshape(flat, width))
        for group, (_, end) in enumerate(swap_groups):
            if end == index - (ticks - micros) + 1:
                at = 3 + group
                if hops:
                    stores[at], arrived[index + 1] = lax.optimization_barrier((stores[at], arrived[index + 1]))
                if got:
                    stores[at], got[-1] = lax.optimization_barrier((stores[at], got[-1]))
                got.append(swap(stores[at]))
    grads_in, upstream, d_store, *s_stores = stores

    grad_scale = (flat * n_data) ** (-0.5)
    parts = []
    part_specs = []
    for own, part in zip(s_stores[::-1], got):
        count = part.shape[0]
        parts += [own, part, part]
        part_specs += [
            pl.BlockSpec((count, 1, tokens, width), lambda j, p: (0, 0, 0, 0)),
            pl.BlockSpec((count, 1, tokens, width), lambda j, p: (0, 0, 0, 0)),
            pl.BlockSpec((count, 1, tokens, block), lambda j, p: (0, 1, 0, j)),
        ]
    terms = pl.pallas_call(
        functools.partial(weight_grads_kernel, grad_scale),
        cost_estimate=cost(9),
        out_shape=jax.ShapeDtypeStruct((half, 2 * width), BF),
        grid_spec=pltpu.PrefetchScalarGridSpec(
            num_scalar_prefetch=1,
            grid=(halves,),
            in_specs=[
                pl.BlockSpec((flat, block), lambda j, p: (0, 2 * j + p[0])),
                pl.BlockSpec((flat, block), lambda j, p: (0, j)),
                pl.BlockSpec((flat, block), lambda j, p: (0, 2 * j + p[0])),
                pl.BlockSpec((flat, width), lambda j, p: (0, 0)),
                pl.BlockSpec((flat, width), lambda j, p: (0, 0)),
                *part_specs,
            ],
            out_specs=pl.BlockSpec((block, 2 * width), lambda j, p: (j, 0)),
        ),
        compiler_params=params(),
    )(
        parity[None].astype(jnp.int32),
        inputs_all.reshape(flat, model),
        inputs_got,
        upstream.reshape(flat, model),
        attended.reshape(flat, width),
        attended_got,
        *parts,
    )
    d_heads = exchange(d_store) if head_major else exchange(by_heads(d_store))
    d_heads = d_heads.reshape(n_data, q_rows, slice_w)
    terms, d_heads = lax.optimization_barrier((terms, d_heads))
    shares = lax.psum_scatter(
        terms,
        "dp",
        scatter_dimension=0,
        tiled=True,
        axis_index_groups=[list(range(p, n_data, 2)) for p in range(2)],
    )

    ids_all = sliced[:, q_rows + kv_rows :, 0].astype(jnp.int32).reshape(n_data, micros, spans, K_NBR)
    ids_all = jnp.moveaxis(ids_all, 0, 1).reshape(micros, n_data * spans, K_NBR)
    owner_all = ids_all // blk_dev
    reader_all = (jnp.arange(n_data * spans, dtype=jnp.int32) // spans)[None, :, None]
    hit_owner = owner_all[..., None] == jnp.arange(n_data, dtype=jnp.int32)
    list_r = jnp.take(send_list, reader_all[0, :, 0], axis=1).T[None, :, None, :]
    count_r = jnp.take(send_counts, reader_all[0, :, 0], axis=1).T[None, :, None, :]
    block_all = owner_all * blk_dev + jnp.sum(jnp.where(hit_owner, list_r, 0), axis=-1)
    mask_all = jnp.sum(jnp.where(hit_owner, count_r, 0), axis=-1)
    blocks = n_data * blk_dev
    block_grads = pl.pallas_call(
        functools.partial(block_grads_kernel, micros, blk_dev),
        cost_estimate=cost(37),
        out_shape=jax.ShapeDtypeStruct((blocks, 2, NBR_LEN, slice_w), BF),
        grid_spec=pltpu.PrefetchScalarGridSpec(
            num_scalar_prefetch=2,
            grid=(n_data,),
            in_specs=[
                pl.BlockSpec((1, q_rows, slice_w), lambda i, a, b: (i, 0, 0)),
                pl.BlockSpec((1, q_rows, slice_w), lambda i, a, b: (i, 0, 0)),
                pl.BlockSpec((n_data, kv_rows, slice_w), lambda i, a, b: (0, q_rows // kv_rows, 0)),
            ],
            out_specs=pl.BlockSpec((blocks, 2, NBR_LEN, slice_w), lambda i, a, b: (0, 0, 0, 0)),
            scratch_shapes=[pltpu.VMEM((blocks, 2, NBR_LEN, slice_w), F32)],
        ),
        compiler_params=params(),
    )(block_all.reshape(-1).astype(jnp.int32), mask_all.reshape(-1).astype(jnp.int32), sliced, d_heads, sliced)
    returned = exchange(block_grads.reshape(n_data, blk_dev, 2, NBR_LEN, slice_w))
    kv_grads = jnp.moveaxis(returned, 0, -2).reshape(blk_dev, 2, NBR_LEN, width)
    return (
        grads_in[None],
        shares[None, :, :width],
        shares[None, :, width:],
        kv_grads[None],
    )


def solution(mesh):
    in_specs = (
        P("section", None, "dp", None),
        P(None, "dp", None),
        P("section", None, None),
        P("section", None, None),
        P("section", "dp", None, None, None),
        P(None, "dp", None),
        P(),
        P(),
    )
    out_specs = (
        P("section", None, "dp", None),
        P("section", "dp", None),
        P("section", "dp", None),
        P("section", "dp", None, None, None),
    )
    return jax.shard_map(body, mesh=mesh, in_specs=in_specs, out_specs=out_specs, check_vma=False)
```
